32 devices in a mesh: user: 4 (over z), ctx: 2 (over y), head: 4 (over x, core).
Axes of the slice: x: 2, y: 2, z: 4, core: 2. Of those that a mesh axis runs over, the one named last changes fastest.
Arguments:
- catalog: bfloat16 [2048, 1024], P('user'), may hold values from -6 to 6
- cand_owner: int32 [4, 512, 1], P('user', 'ctx'), may hold values from 0 to 3; in each aligned block of 256 rows (0 to 255, 256 to 511, ..., all dimensions but the last counted through in order) at most 128 rows name the same one
- cand_row: int32 [4, 512], P('user', 'ctx'), may hold values from 0 to 511
- hist_len: int32 [4], P('user'), may hold values from 768 to 3072, as said below
- proj_weight: bfloat16 [1024, 2, 1024], P(None, None, 'head'), may hold values from -0.1875 to 0.1875
- keys: bfloat16 [4, 3072, 1024], P('user', 'ctx', 'head'), may hold values from -6 to 6
- values: bfloat16 [4, 3072, 1024], P('user', 'ctx', 'head'), may hold values from -640 to 640
- out_weight: bfloat16 [1024, 1024], P('head'), may hold values from -0.1875 to 0.1875
Outputs:
- ranked: bfloat16 [4, 512, 1024], P('user', 'ctx', 'head')
The draws below stay inside these ranges and needn't reach their ends.
Inputs may be any that keep to these rules, and one draw needn't show every extreme that they name: `cand_owner`: within each aligned block of 256 shortlisted items of one user (one ctx index), at most 128 are owned by the same catalog shard. `hist_len`: at least one user has all 3072 events.
All inputs are finite; a program needn't handle non-finite values.
Results may differ from the reference program's by a relative error of at most 0.0071.
Values may be sent and summed in bfloat16 or wider, within the bound.
No kernel may reach another device: no remote copies, remote signals or barrier semaphores. Data moves between devices by JAX's collectives and lax.ppermute only.
A program may use at most 64 MiB of HBM per device.

```python
import math
import jax
import jax.numpy as jnp
import numpy as np
from jax import lax

D = 1024
HEAD = 128
CAND_DEV = 256
HIST_DEV = 1536
ROWS_DEV = 512
USERS = 4
CAND = 512
HIST = 3072
ITEMS = 2048
CAP = 128
N_USER = 4
N_CTX = 2


def draw_hist_len(key, part):
    first_key, second_key = jax.random.split(jax.random.fold_in(key, 17))
    lengths = jax.random.randint(first_key, (USERS,), HIST // 4, HIST + 1)
    chosen = jax.random.randint(second_key, (), 0, USERS)
    return jnp.where(jnp.arange(USERS) == chosen, HIST, lengths).astype(jnp.int32)


def place_ends(array, key, smallest, top_value):
    longest = array.shape.index(max(array.shape))
    spots = []
    for shift in (0, 1):
        where = [jax.random.randint(jax.random.fold_in(key, axis), (), 0, length) for axis, length in enumerate(array.shape)]
        where[longest] = (where[longest] + shift) % array.shape[longest]
        spots.append(tuple(where))
    return array.at[spots[0]].set(smallest).at[spots[1]].set(top_value)


def steps_of(rng, extent, cuts, low, top_value):
    gain = 1.0
    for position, blocks in cuts:
        steps = jax.random.uniform(jax.random.fold_in(jax.random.fold_in(rng, 6), position), (blocks,), jnp.float32, low / len(cuts), top_value / len(cuts))
        gain = gain * jnp.repeat(jnp.exp(steps), extent[position] // blocks).reshape((-1,) + (1,) * (len(extent) - 1 - position))
    return gain


def assign_block(key, own, number, rows, amount, top, bound, skew):
    sequence = jax.random.permutation(key, amount)
    crowded, common = portions_of(amount, rows * top, bound, skew, True), portions_of(amount, rows * top, bound, skew, False)
    places = jnp.arange(amount)

    def named(tallies, offset_by):
        used = int((tallies > 0).sum())
        fixed = max(1, used // 4)
        moved = fixed + (places - fixed + offset_by * (used - fixed)) % max(1, amount - fixed)
        return jnp.zeros((amount,), jnp.int32).at[sequence[jnp.where(places < fixed, places, moved)]].set(jnp.asarray(tallies, jnp.int32))

    tallies = jnp.where(number % 4 == 0, named(crowded, number // 4), named(common, number - number // 4 - 1))
    mixed = jax.random.permutation(jax.random.fold_in(own, 3), amount)
    donor, sink = mixed[0:amount // 2 * 2:2], mixed[1:amount // 2 * 2:2]
    slack = jnp.minimum(tallies[donor] - 1, bound - tallies[sink]) // 2
    slack = jnp.where((donor == sequence[0]) | (sink == sequence[0]) | (tallies[sink] == 0), 0, jnp.maximum(slack, 0))
    moved = jax.random.randint(jax.random.fold_in(own, 4), (amount // 2,), 0, 1 << 20) % (slack + 1)
    tallies = tallies.at[donor].add(-moved).at[sink].add(moved)
    labels = jnp.searchsorted(jnp.cumsum(tallies), jnp.arange(rows * top), side="right").astype(jnp.int32)
    grid = labels.reshape(top, rows).T
    grid = grid[jax.random.permutation(jax.random.fold_in(own, 1), rows)]
    offset_by = jax.random.randint(jax.random.fold_in(own, 2), (rows, 1), 0, top)
    return jnp.take_along_axis(grid, (jnp.arange(top)[None, :] + offset_by) % top, axis=1)


def portions_of(amount, total, limit, slope, full):
    weights = [(1 << 20) // math.isqrt(grade ** slope) + 1 for grade in range(1, amount + 1)]
    largest = limit if full else min(limit, max(-(-total // amount), total * weights[0] // sum(weights)))
    least = 1 if total - largest >= amount - 1 else 0
    counts, rest = [largest] + [least] * (amount - 1), total - largest - least * (amount - 1)
    while rest > 0:
        movable = [i for i in range(1, amount) if counts[i] < largest] or [i for i in range(1, amount) if counts[i] < limit]
        mass, left = sum([weights[i] for i in movable]), rest
        for i in movable:
            extra = min(limit - counts[i], max(1, left * weights[i] // mass), rest)
            counts[i] = counts[i] + extra
            rest = rest - extra
    return np.array(counts)


def noise(stream_key, dims, deviation, limit, shards=(), kind=jnp.bfloat16):
    values = jax.random.normal(stream_key, dims, jnp.float32) * deviation
    if len(shards) > 0:
        values = steps_of(stream_key, dims, shards, -0.22, 0.18) * values
    return jnp.clip(values, min=-limit, max=limit).astype(kind)


def setup_inputs(seed: int = 0) -> dict:
    arg_keys = jax.random.split(jax.random.key(seed), 9)
    catalog = noise(arg_keys[0], (ITEMS, D), 1.0, 6.0, ((0, 4),))
    cand_owner_keys = jax.random.split(jax.random.fold_in(arg_keys[1], 1), USERS * CAND // CAND_DEV)
    cand_owner_turns = jax.random.permutation(jax.random.fold_in(arg_keys[1], 3), USERS * CAND // CAND_DEV)
    cand_owner = jax.vmap(lambda own, number: assign_block(jax.random.fold_in(arg_keys[1], 2), own, number, CAND_DEV, N_USER, 1, CAP, 1))(cand_owner_keys, cand_owner_turns).reshape((USERS, CAND, 1))
    cand_row = place_ends(jax.random.randint(arg_keys[2], (USERS, CAND), 0, ROWS_DEV), jax.random.fold_in(arg_keys[2], 1), 0, ROWS_DEV - 1).astype(jnp.int32)
    hist_len = draw_hist_len(jax.random.fold_in(arg_keys[8], 71), 0)
    proj_weight = noise(arg_keys[4], (D, 2, D), D ** -0.5, 0.1875, ((2, 4),))
    keys = noise(arg_keys[5], (USERS, HIST, D), 1.0, 6.0, ((0, 4), (1, 2), (2, 4)))
    values = noise(arg_keys[6], (USERS, HIST, D), (2 * (HIST_DEV * N_CTX) ** 0.5), 640.0, ((0, 4), (1, 2), (2, 4)))
    out_weight = noise(arg_keys[7], (D, D), D ** -0.5, 0.1875, ((0, 4),))
    return {"catalog": catalog, "cand_owner": cand_owner, "cand_row": cand_row, "hist_len": hist_len, "proj_weight": proj_weight, "keys": keys, "values": values, "out_weight": out_weight}


def attend_user(query_rows, key_rows, value_rows, length):
    head_count = D // HEAD
    query_heads = query_rows.astype(jnp.float32).reshape(CAND, head_count, HEAD)
    length_float = length.astype(jnp.float32)

    def add_block(running, block_index):
        row_start = (block_index * HIST_DEV).astype(jnp.int32)
        key_block = lax.dynamic_slice_in_dim(key_rows, row_start, HIST_DEV, 0).astype(jnp.float32).reshape(HIST_DEV, head_count, HEAD)
        value_block = lax.dynamic_slice_in_dim(value_rows, row_start, HIST_DEV, 0).astype(jnp.float32).reshape(HIST_DEV, head_count, HEAD)
        scores = jnp.einsum("rhc,nhc->rhn", query_heads, key_block) * (HEAD ** -0.5)
        places = row_start + jnp.arange(HIST_DEV, dtype=jnp.int32)
        weights = jnp.where(places[None, None, :] < length, jax.nn.silu(scores) / length_float, 0.0).astype(jnp.bfloat16)
        weights = lax.optimization_barrier(weights).astype(jnp.float32)
        return running + jnp.einsum("rhn,nhc->rhc", weights, value_block), None

    running, unused = lax.scan(add_block, jnp.zeros((CAND, head_count, HEAD), jnp.float32), jnp.arange(N_CTX, dtype=jnp.int32))
    return running.reshape(CAND, D)


def reference(catalog, cand_owner, cand_row, hist_len, proj_weight, keys, values, out_weight):
    item_ids = (cand_owner[:, :, 0].astype(jnp.int32) * ROWS_DEV + cand_row.astype(jnp.int32)).reshape(-1)
    item_rows = jnp.take(catalog, item_ids, axis=0)
    pre_act = jnp.dot(item_rows, proj_weight.reshape(D, 2 * D), preferred_element_type=jnp.float32)
    projected = lax.optimization_barrier(jax.nn.silu(pre_act).astype(jnp.bfloat16)).reshape(USERS, CAND, 2, D)
    queries = projected[:, :, 0, :]
    gates = projected[:, :, 1, :]
    attended = lax.map(lambda packed: attend_user(packed[0], packed[1], packed[2], packed[3]), (queries, keys, values, hist_len))
    gated_rows = (attended * gates.astype(jnp.float32)).astype(jnp.bfloat16)
    ranked = jnp.dot(gated_rows.reshape(USERS * CAND, D), out_weight, preferred_element_type=jnp.float32)
    return ranked.astype(jnp.bfloat16).reshape(USERS, CAND, D)
```

```python
import functools

import jax
import jax.numpy as jnp
from jax import lax
from jax.experimental import pallas as pl
from jax.experimental.pallas import tpu as pltpu
from jax.sharding import PartitionSpec as P

HEAD = 128


def attend_block(query_rows, key_rows, value_rows, offset, length):
    row_total = query_rows.shape[0]
    key_total = key_rows.shape[0]
    head_count = query_rows.shape[1] // HEAD
    query_heads = query_rows.reshape(row_total, head_count, HEAD)
    key_heads = key_rows.reshape(key_total, head_count, HEAD)
    value_heads = value_rows.reshape(key_total, head_count, HEAD)
    scores = jnp.einsum(
        "rhc,nhc->rhn", query_heads, key_heads, preferred_element_type=jnp.float32
    ) * HEAD ** (-0.5)
    places = offset + jnp.arange(key_total, dtype=jnp.int32)
    weights = jnp.where(
        places[None, None, :] < length, jax.nn.silu(scores) / length.astype(jnp.float32), 0.0
    ).astype(jnp.bfloat16)
    mixed_rows = jnp.einsum(
        "rhn,nhc->rhc", weights, value_heads, preferred_element_type=jnp.float32
    )
    return mixed_rows.reshape(row_total, head_count * HEAD)


def event_split(catalog, cand_owner, cand_row, hist_len, proj_weight, keys, values, out_weight):
    user_count = lax.axis_size("user")
    owners = cand_owner[0, :, 0]
    wanted = cand_row[0]
    cand_count = wanted.shape[0]
    slot_count = 2 * cand_count // user_count
    model_width = catalog.shape[1]
    col_share = proj_weight.shape[2]
    owner_hot = (owners[:, None] == jnp.arange(user_count, dtype=jnp.int32)[None, :]).astype(
        jnp.int32
    )
    rank_in = jnp.sum(jnp.cumsum(owner_hot, axis=0) * owner_hot, axis=1) - 1
    places = owners * slot_count + rank_in
    request = (
        jnp.zeros((user_count * slot_count,), jnp.int32)
        .at[places]
        .set(wanted)
        .reshape(user_count, slot_count)
    )
    weight_flat = proj_weight.reshape(model_width, 2 * col_share)
    asked_ids = lax.all_to_all(request, "user", split_axis=0, concat_axis=0, tiled=True)
    picked = jax.nn.silu(
        jnp.dot(
            jnp.take(catalog, asked_ids.reshape(-1), axis=0),
            weight_flat,
            preferred_element_type=jnp.float32,
        )
    ).astype(jnp.bfloat16)
    served = picked.reshape(asked_ids.shape[0], asked_ids.shape[1], 2 * col_share)
    returned = lax.all_to_all(served, "user", split_axis=0, concat_axis=0, tiled=True)
    own_rows = jnp.take(returned.reshape(user_count * slot_count, 2 * col_share), places, axis=0)
    queries = own_rows[:, :col_share]
    gates = own_rows[:, col_share:]
    length = hist_len[0]
    key_rows = keys[0]
    value_rows = values[0]
    all_queries = lax.all_gather(queries, "ctx", axis=0, tiled=True)
    offset = lax.axis_index("ctx") * key_rows.shape[0]
    attended = lax.psum_scatter(
        attend_block(all_queries, key_rows, value_rows, offset, length),
        "ctx",
        scatter_dimension=0,
        tiled=True,
    )
    gated_rows = (attended * gates.astype(jnp.float32)).astype(jnp.bfloat16)
    partials = jnp.dot(gated_rows, out_weight, preferred_element_type=jnp.float32)
    ranked = lax.psum_scatter(partials, "head", scatter_dimension=1, tiled=True).astype(
        jnp.bfloat16
    )
    return ranked.reshape(1, cand_count, col_share)


def swap(x, axis, k):
    return lax.ppermute(x, axis, [(i, i ^ k) for i in range(lax.axis_size(axis))])


def silu(x):
    half = 0.5 * x
    return half + half * jnp.tanh(half)


KEY_BLOCK = 512


def attention_kernel(user_count, ctx_count, scalars, ids_ref, *refs):
    query_refs = refs[:user_count]
    gate_refs = refs[user_count : 2 * user_count]
    key_refs = refs[2 * user_count : 2 * user_count + ctx_count]
    value_refs = refs[2 * user_count + ctx_count : 2 * user_count + 2 * ctx_count]
    out_ref = refs[-1]
    length, user, ctx = scalars[0], scalars[1], scalars[2]
    shard_rows, width = query_refs[0].shape
    ids = ids_ref[...]
    item_count = ids.shape[0]
    query = jnp.zeros((item_count, width), jnp.float32)
    gate = jnp.zeros((item_count, width), jnp.float32)
    row_of = lax.broadcasted_iota(jnp.int32, (item_count, shard_rows), 1)
    for k in range(user_count):
        hot = (ids - (user ^ k) * shard_rows == row_of).astype(jnp.bfloat16)
        query += jnp.dot(hot, query_refs[k][...], preferred_element_type=jnp.float32)
        gate += jnp.dot(hot, gate_refs[k][...], preferred_element_type=jnp.float32)
    query = query.astype(jnp.bfloat16)
    event_count = value_refs[0].shape[0]
    own = pl.ds(pl.multiple_of(ctx * width, width), width)
    scale = 0.5 * HEAD ** (-0.5)
    scale_len = scale / jnp.full((1, 1), length, jnp.int32).astype(jnp.float32)
    for head in range(width // HEAD):
        cols = slice(head * HEAD, (head + 1) * HEAD)
        total = jnp.zeros((item_count, HEAD), jnp.float32)
        for k in range(ctx_count):
            first = (ctx ^ k) * event_count
            for start in range(0, event_count, KEY_BLOCK):
                rows = slice(start, start + KEY_BLOCK)
                if k == 0:
                    at = pl.ds(pl.multiple_of(ctx * width + head * HEAD, HEAD), HEAD)
                    key, value = key_refs[0][rows, at], value_refs[0][rows, at]
                else:
                    key, value = key_refs[k][rows, cols], value_refs[k][rows, cols]
                place = first + start + lax.broadcasted_iota(jnp.int32, value.shape, 0)
                value = jnp.where(place < length, value, jnp.zeros_like(value))
                raw = lax.dot_general(
                    query[:, cols],
                    key,
                    (((1,), (1,)), ((), ())),
                    preferred_element_type=jnp.float32,
                )
                lead = raw * scale_len
                weights = (lead + lead * jnp.tanh(raw * scale)).astype(jnp.bfloat16)
                total += jnp.dot(weights, value, preferred_element_type=jnp.float32)
        out_ref[:, cols] = (total * gate[:, cols]).astype(out_ref.dtype)


def attend(scalars, ids, queries, gates, key_parts, value_parts):
    item_count, width = ids.shape[0], queries[0].shape[1]
    user_count, ctx_count = len(queries), len(key_parts)
    events = ctx_count * value_parts[0].shape[0]
    vmem = pl.BlockSpec(memory_space=pltpu.VMEM)
    operands = (ids, *queries, *gates, *key_parts, *value_parts)
    return pl.pallas_call(
        functools.partial(attention_kernel, user_count, ctx_count),
        out_shape=jax.ShapeDtypeStruct((item_count, width), jnp.bfloat16),
        in_specs=[pl.BlockSpec(memory_space=pltpu.SMEM)] + [vmem] * len(operands),
        out_specs=vmem,
        compiler_params=pltpu.CompilerParams(vmem_limit_bytes=24 << 20),
        cost_estimate=pl.CostEstimate(
            flops=4 * item_count * events * width,
            transcendentals=item_count * events * (width // HEAD),
            bytes_accessed=4 * events * width,
        ),
    )(scalars, *operands)


def project_kernel(head_count, ctx_count, scalars, *refs):
    pieces = refs[: head_count * ctx_count]
    weights = refs[head_count * ctx_count : head_count * (ctx_count + 1)]
    out_ref = refs[-1]
    ctx = scalars[2]
    width = pieces[0].shape[1]
    total = jnp.zeros(out_ref.shape, jnp.float32)
    for j in range(head_count):
        for k in range(ctx_count):
            rows = pl.ds(pl.multiple_of((ctx ^ k) * width, width), width)
            total += jnp.dot(
                pieces[j * ctx_count + k][...],
                weights[j][rows, :],
                preferred_element_type=jnp.float32,
            )
    out_ref[...] = total.astype(out_ref.dtype)


def project_out(scalars, pieces, weights):
    head_count = len(weights)
    item_count, cols = pieces[0].shape[0], weights[0].shape[1]
    vmem = pl.BlockSpec(memory_space=pltpu.VMEM)
    operands = (*pieces, *weights)
    return pl.pallas_call(
        functools.partial(project_kernel, head_count, len(pieces) // head_count),
        out_shape=jax.ShapeDtypeStruct((item_count, cols), jnp.bfloat16),
        in_specs=[pl.BlockSpec(memory_space=pltpu.SMEM)] + [vmem] * len(operands),
        out_specs=vmem,
        compiler_params=pltpu.CompilerParams(vmem_limit_bytes=16 << 20),
        cost_estimate=pl.CostEstimate(
            flops=2 * item_count * cols * cols * head_count,
            transcendentals=0,
            bytes_accessed=2 * cols * cols * head_count,
        ),
    )(scalars, *operands)


def head_split(catalog, cand_owner, cand_row, hist_len, proj_weight, keys, values, out_weight):
    user_count, ctx_count = lax.axis_size("user"), lax.axis_size("ctx")
    head_count = lax.axis_size("head")
    user, ctx, head = (lax.axis_index(a) for a in ("user", "ctx", "head"))
    shard_rows = catalog.shape[0]
    col_share = proj_weight.shape[2]
    width = col_share // ctx_count
    key_rows, value_rows = keys[0], values[0]
    cand_count = cand_row.shape[1]
    scalars = jnp.stack([hist_len[0], user, ctx]).astype(jnp.int32)

    key_parts, value_parts = [key_rows], [value_rows]
    for k in range(1, ctx_count):
        at = (ctx ^ k) * width
        key_parts.append(swap(lax.dynamic_slice_in_dim(key_rows, at, width, 1), "ctx", k))
        value_parts.append(swap(lax.dynamic_slice_in_dim(value_rows, at, width, 1), "ctx", k))

    picked = lax.dynamic_slice_in_dim(proj_weight, ctx * width, width, 2)
    queries = [
        silu(jnp.dot(catalog, picked[:, 0], preferred_element_type=jnp.float32)).astype(
            jnp.bfloat16
        )
    ]
    gates = [
        silu(jnp.dot(catalog, picked[:, 1], preferred_element_type=jnp.float32)).astype(
            jnp.bfloat16
        )
    ]
    order = range(user_count - 1, 0, -1)
    fetched = {k: swap(queries[0], "user", k) for k in order}
    queries += [fetched[k] for k in range(1, user_count)]
    fetched = {k: swap(gates[0], "user", k) for k in order}
    gates += [fetched[k] for k in range(1, user_count)]

    ids = (cand_owner[0, :, 0] * shard_rows + cand_row[0])[:, None]
    ids_of = [ids] + [swap(ids, "ctx", k) for k in range(1, ctx_count)]

    weights = [lax.dynamic_slice_in_dim(out_weight, head * col_share, col_share, 1)]
    for j in range(1, head_count):
        part = lax.dynamic_slice_in_dim(out_weight, (head ^ j) * col_share, col_share, 1)
        weights.append(swap(part, "head", j))

    pieces = [[None] * ctx_count for _ in range(head_count)]
    for k in range(ctx_count - 1, 0, -1):
        gated = attend(scalars, ids_of[k], queries, gates, key_parts, value_parts)
        pieces[0][k] = swap(gated, "ctx", k)
    pieces[0][0] = attend(scalars, ids_of[0], queries, gates, key_parts, value_parts)
    for k in range(ctx_count):
        for j in range(head_count - 1, 0, -1):
            pieces[j][k] = swap(pieces[0][k], "head", j)
    ranked = project_out(scalars, [p for row in pieces for p in row], weights)
    return ranked.reshape(1, cand_count, col_share)


def whole_heads(mesh, proj_weight):
    sizes = [mesh.shape[a] for a in ("user", "ctx", "head")]
    heads = proj_weight.shape[2] // mesh.shape["head"] // HEAD
    return all(n & (n - 1) == 0 for n in sizes) and heads % mesh.shape["ctx"] == 0


def solution(mesh):
    def run(catalog, cand_owner, cand_row, hist_len, proj_weight, keys, values, out_weight):
        per_device = head_split if whole_heads(mesh, proj_weight) else event_split
        return jax.shard_map(
            per_device,
            mesh=mesh,
            in_specs=(
                P("user", None),
                P("user", "ctx", None),
                P("user", "ctx"),
                P("user"),
                P(None, None, "head"),
                P("user", "ctx", "head"),
                P("user", "ctx", "head"),
                P("head", None),
            ),
            out_specs=P("user", "ctx", "head"),
            check_vma=False,
        )(catalog, cand_owner, cand_row, hist_len, proj_weight, keys, values, out_weight)

    return run
```

```python
import functools

import jax
import jax.numpy as jnp
from jax import lax
from jax.experimental import pallas as pl
from jax.experimental.pallas import tpu as pltpu
from jax.sharding import PartitionSpec as P

HEAD = 128


def attend_block(query_rows, key_rows, value_rows, offset, length):
    row_total = query_rows.shape[0]
    key_total = key_rows.shape[0]
    head_count = query_rows.shape[1] // HEAD
    query_heads = query_rows.reshape(row_total, head_count, HEAD)
    key_heads = key_rows.reshape(key_total, head_count, HEAD)
    value_heads = value_rows.reshape(key_total, head_count, HEAD)
    scores = jnp.einsum(
        "rhc,nhc->rhn", query_heads, key_heads, preferred_element_type=jnp.float32
    ) * HEAD ** (-0.5)
    places = offset + jnp.arange(key_total, dtype=jnp.int32)
    weights = jnp.where(
        places[None, None, :] < length, jax.nn.silu(scores) / length.astype(jnp.float32), 0.0
    ).astype(jnp.bfloat16)
    mixed_rows = jnp.einsum(
        "rhn,nhc->rhc", weights, value_heads, preferred_element_type=jnp.float32
    )
    return mixed_rows.reshape(row_total, head_count * HEAD)


def event_split(catalog, cand_owner, cand_row, hist_len, proj_weight, keys, values, out_weight):
    user_count = lax.axis_size("user")
    owners = cand_owner[0, :, 0]
    wanted = cand_row[0]
    cand_count = wanted.shape[0]
    slot_count = 2 * cand_count // user_count
    model_width = catalog.shape[1]
    col_share = proj_weight.shape[2]
    owner_hot = (owners[:, None] == jnp.arange(user_count, dtype=jnp.int32)[None, :]).astype(
        jnp.int32
    )
    rank_in = jnp.sum(jnp.cumsum(owner_hot, axis=0) * owner_hot, axis=1) - 1
    places = owners * slot_count + rank_in
    request = (
        jnp.zeros((user_count * slot_count,), jnp.int32)
        .at[places]
        .set(wanted)
        .reshape(user_count, slot_count)
    )
    weight_flat = proj_weight.reshape(model_width, 2 * col_share)
    asked_ids = lax.all_to_all(request, "user", split_axis=0, concat_axis=0, tiled=True)
    picked = jax.nn.silu(
        jnp.dot(
            jnp.take(catalog, asked_ids.reshape(-1), axis=0),
            weight_flat,
            preferred_element_type=jnp.float32,
        )
    ).astype(jnp.bfloat16)
    served = picked.reshape(asked_ids.shape[0], asked_ids.shape[1], 2 * col_share)
    returned = lax.all_to_all(served, "user", split_axis=0, concat_axis=0, tiled=True)
    own_rows = jnp.take(returned.reshape(user_count * slot_count, 2 * col_share), places, axis=0)
    queries = own_rows[:, :col_share]
    gates = own_rows[:, col_share:]
    length = hist_len[0]
    key_rows = keys[0]
    value_rows = values[0]
    all_queries = lax.all_gather(queries, "ctx", axis=0, tiled=True)
    offset = lax.axis_index("ctx") * key_rows.shape[0]
    attended = lax.psum_scatter(
        attend_block(all_queries, key_rows, value_rows, offset, length),
        "ctx",
        scatter_dimension=0,
        tiled=True,
    )
    gated_rows = (attended * gates.astype(jnp.float32)).astype(jnp.bfloat16)
    partials = jnp.dot(gated_rows, out_weight, preferred_element_type=jnp.float32)
    ranked = lax.psum_scatter(partials, "head", scatter_dimension=1, tiled=True).astype(
        jnp.bfloat16
    )
    return ranked.reshape(1, cand_count, col_share)


def swap(x, axis, k):
    return lax.ppermute(x, axis, [(i, i ^ k) for i in range(lax.axis_size(axis))])


def silu(x):
    half = 0.5 * x
    return half + half * jnp.tanh(half)


KEY_BLOCK = 512


def one_hot(condition):
    return jnp.where(condition, 1.0, 0.0).astype(jnp.bfloat16)


def serve_kernel(user_count, slot_count, scalars, ids_ref, rows_ref, slots_ref, ranks_ref, *out_refs):
    user, ctx = scalars[1], scalars[2]
    shard_rows = rows_ref.shape[0]
    width = out_refs[0].shape[1]
    ids = ids_ref[...]
    item_count = ids.shape[1]
    served = ids - user * shard_rows
    mine = [one_hot((served >= 0) & (served < shard_rows))]
    for k in range(user_count):
        own = ids[0:1] - (user ^ k) * shard_rows
        mine.append(one_hot((own >= 0) & (own < shard_rows)))
    mine = jnp.concatenate(mine, axis=0)
    before = one_hot(
        lax.broadcasted_iota(jnp.int32, (item_count, item_count), 0)
        < lax.broadcasted_iota(jnp.int32, (item_count, item_count), 1)
    )
    rank = jnp.dot(mine, before, preferred_element_type=jnp.float32)
    asked = mine[user_count:].astype(jnp.float32)
    shard = lax.broadcasted_iota(jnp.int32, asked.shape, 0).astype(jnp.float32)
    ranks_ref[0:1] = jnp.sum(asked * rank[user_count:], axis=0, keepdims=True)
    ranks_ref[1:2] = jnp.sum(asked * shard, axis=0, keepdims=True)
    served = jnp.clip(served, 0, shard_rows - 1)
    slot = lax.broadcasted_iota(jnp.int32, (slot_count, item_count), 0).astype(jnp.float32)
    row = lax.broadcasted_iota(jnp.int32, (slot_count, shard_rows), 1)
    cols = pl.ds(pl.multiple_of(ctx * width, width), width)
    for k in range(user_count):
        place = jnp.where(mine[k : k + 1] > 0, rank[k : k + 1], -1.0)
        parts = jnp.concatenate([served[k : k + 1] >> 8, served[k : k + 1] & 255], axis=0)
        found = lax.dot_general(
            one_hot(slot == place),
            parts.astype(jnp.float32).astype(jnp.bfloat16),
            (((1,), (1,)), ((), ())),
            preferred_element_type=jnp.float32,
        )
        at = (found[:, 0:1] * 256.0 + found[:, 1:2]).astype(jnp.int32)
        slots_ref[:, k : k + 1] = at
        if k > 0:
            out_refs[k - 1][...] = jnp.dot(
                one_hot(row == at), rows_ref[:, cols], preferred_element_type=jnp.float32
            ).astype(jnp.bfloat16)


def serve(scalars, ids, rows, slot_count, width):
    user_count, item_count = ids.shape
    vmem = pl.BlockSpec(memory_space=pltpu.VMEM)
    return pl.pallas_call(
        functools.partial(serve_kernel, user_count, slot_count),
        out_shape=[
            jax.ShapeDtypeStruct((slot_count, user_count), jnp.int32),
            jax.ShapeDtypeStruct((2, item_count), jnp.float32),
        ]
        + [jax.ShapeDtypeStruct((slot_count, width), jnp.bfloat16)] * (user_count - 1),
        in_specs=[pl.BlockSpec(memory_space=pltpu.SMEM), vmem, vmem],
        out_specs=[vmem] * (user_count + 1),
        compiler_params=pltpu.CompilerParams(vmem_limit_bytes=16 << 20),
        cost_estimate=pl.CostEstimate(
            flops=2 * user_count * slot_count * rows.shape[0] * width,
            transcendentals=0,
            bytes_accessed=2 * rows.shape[0] * width,
        ),
    )(scalars, ids, rows)


def serve_rest_kernel(user_count, scalars, slots_ref, ranks_ref, rows_ref, plan_ref, query_ref, *out_refs):
    ctx = scalars[2]
    shard_rows, both = rows_ref.shape
    slot_count, width = query_ref.shape
    query_cols = pl.ds(pl.multiple_of(ctx * width, width), width)
    gate_cols = pl.ds(pl.multiple_of(both // 2 + ctx * width, width), width)
    row = lax.broadcasted_iota(jnp.int32, (slot_count, shard_rows), 1)
    for k in range(user_count):
        hot = one_hot(row == slots_ref[:, k : k + 1])
        out_refs[k][...] = jnp.dot(
            hot, rows_ref[:, gate_cols], preferred_element_type=jnp.float32
        ).astype(jnp.bfloat16)
        if k == 0:
            query_ref[...] = jnp.dot(
                hot, rows_ref[:, query_cols], preferred_element_type=jnp.float32
            ).astype(jnp.bfloat16)
    item_count = ranks_ref.shape[1]
    same = one_hot(
        lax.broadcasted_iota(jnp.int32, (item_count, item_count), 0)
        == lax.broadcasted_iota(jnp.int32, (item_count, item_count), 1)
    )
    found = lax.dot_general(
        same,
        ranks_ref[...].astype(jnp.bfloat16),
        (((1,), (1,)), ((), ())),
        preferred_element_type=jnp.float32,
    )
    plan_ref[...] = (found[:, 0:1] + found[:, 1:2] * slot_count).astype(jnp.int32)


def serve_rest(scalars, slots, ranks, rows, width):
    slot_count, user_count = slots.shape
    vmem = pl.BlockSpec(memory_space=pltpu.VMEM)
    return pl.pallas_call(
        functools.partial(serve_rest_kernel, user_count),
        out_shape=[jax.ShapeDtypeStruct((ranks.shape[1], 1), jnp.int32)]
        + [jax.ShapeDtypeStruct((slot_count, width), jnp.bfloat16)] * (user_count + 1),
        in_specs=[pl.BlockSpec(memory_space=pltpu.SMEM), vmem, vmem, vmem],
        out_specs=[vmem] * (user_count + 2),
        compiler_params=pltpu.CompilerParams(vmem_limit_bytes=16 << 20),
        cost_estimate=pl.CostEstimate(
            flops=2 * user_count * slot_count * rows.shape[0] * width,
            transcendentals=0,
            bytes_accessed=2 * rows.shape[0] * width,
        ),
    )(scalars, slots, ranks, rows)


def pick(plan, slot_refs):
    slot_count, width = slot_refs[0].shape
    slot = lax.broadcasted_iota(jnp.int32, (plan.shape[0], slot_count), 1)
    total = jnp.zeros((plan.shape[0], width), jnp.float32)
    for k, ref in enumerate(slot_refs):
        total += jnp.dot(
            one_hot(slot == plan - k * slot_count), ref[...], preferred_element_type=jnp.float32
        )
    return total


def attention_kernel(group, user_count, ctx_count, scalars, plan_ref, *refs):
    query_refs = refs[:user_count]
    key_refs = refs[user_count : user_count + ctx_count]
    value_refs = refs[user_count + ctx_count : user_count + 2 * ctx_count]
    out_ref = refs[-1]
    length, ctx = scalars[0], scalars[2]
    item_count, width = out_ref.shape
    plan = plan_ref[group * item_count : (group + 1) * item_count, :]
    query = pick(plan, query_refs).astype(jnp.bfloat16)
    event_count = value_refs[0].shape[0]
    scale = 0.5 * HEAD ** (-0.5)
    scale_len = scale / jnp.full((1, 1), length, jnp.int32).astype(jnp.float32)
    for head in range(width // HEAD):
        cols = slice(head * HEAD, (head + 1) * HEAD)
        total = jnp.zeros((item_count, HEAD), jnp.float32)
        for k in range(ctx_count):
            first = (ctx ^ k) * event_count
            for start in range(0, event_count, KEY_BLOCK):
                rows = slice(start, start + KEY_BLOCK)
                if k == 0:
                    at = pl.ds(pl.multiple_of(ctx * width + head * HEAD, HEAD), HEAD)
                    key, value = key_refs[0][rows, at], value_refs[0][rows, at]
                else:
                    key, value = key_refs[k][rows, cols], value_refs[k][rows, cols]
                place = first + start + lax.broadcasted_iota(jnp.int32, value.shape, 0)
                value = jnp.where(place < length, value, jnp.zeros_like(value))
                raw = lax.dot_general(
                    query[:, cols],
                    key,
                    (((1,), (1,)), ((), ())),
                    preferred_element_type=jnp.float32,
                )
                lead = raw * scale_len
                weights = (lead + lead * jnp.tanh(raw * scale)).astype(jnp.bfloat16)
                total += jnp.dot(weights, value, preferred_element_type=jnp.float32)
        out_ref[:, cols] = total


def attend(scalars, plan, queries, key_parts, value_parts, group):
    slot_count, width = queries[0].shape
    user_count, ctx_count = len(queries), len(key_parts)
    item_count = plan.shape[0] // ctx_count
    events = ctx_count * value_parts[0].shape[0]
    vmem = pl.BlockSpec(memory_space=pltpu.VMEM)
    operands = (plan, *queries, *key_parts, *value_parts)
    return pl.pallas_call(
        functools.partial(attention_kernel, group, user_count, ctx_count),
        out_shape=jax.ShapeDtypeStruct((item_count, width), jnp.float32),
        in_specs=[pl.BlockSpec(memory_space=pltpu.SMEM)] + [vmem] * len(operands),
        out_specs=vmem,
        compiler_params=pltpu.CompilerParams(vmem_limit_bytes=24 << 20),
        cost_estimate=pl.CostEstimate(
            flops=4 * item_count * events * width,
            transcendentals=item_count * events * (width // HEAD),
            bytes_accessed=4 * events * width,
        ),
    )(scalars, *operands)


def gate_kernel(group, plan_ref, attended_ref, *refs):
    gate_refs, out_ref = refs[:-1], refs[-1]
    item_count = out_ref.shape[0]
    plan = plan_ref[group * item_count : (group + 1) * item_count, :]
    out_ref[...] = (attended_ref[...] * pick(plan, gate_refs)).astype(out_ref.dtype)


def gate(plan, attended, gates, group):
    vmem = pl.BlockSpec(memory_space=pltpu.VMEM)
    operands = (plan, attended, *gates)
    return pl.pallas_call(
        functools.partial(gate_kernel, group),
        out_shape=jax.ShapeDtypeStruct(attended.shape, jnp.bfloat16),
        in_specs=[vmem] * len(operands),
        out_specs=vmem,
        compiler_params=pltpu.CompilerParams(vmem_limit_bytes=16 << 20),
        cost_estimate=pl.CostEstimate(
            flops=2 * attended.size * len(gates) * gates[0].shape[0],
            transcendentals=0,
            bytes_accessed=6 * attended.size,
        ),
    )(*operands)


def project_kernel(head_count, ctx_count, scalars, *refs):
    pieces = refs[: head_count * ctx_count]
    weights = refs[head_count * ctx_count : head_count * (ctx_count + 1)]
    out_ref = refs[-1]
    ctx = scalars[2]
    width = pieces[0].shape[1]
    total = jnp.zeros(out_ref.shape, jnp.float32)
    for j in range(head_count):
        for k in range(ctx_count):
            rows = pl.ds(pl.multiple_of((ctx ^ k) * width, width), width)
            total += jnp.dot(
                pieces[j * ctx_count + k][...],
                weights[j][rows, :],
                preferred_element_type=jnp.float32,
            )
    out_ref[...] = total.astype(out_ref.dtype)


def project_out(scalars, pieces, weights):
    head_count = len(weights)
    item_count, cols = pieces[0].shape[0], weights[0].shape[1]
    vmem = pl.BlockSpec(memory_space=pltpu.VMEM)
    operands = (*pieces, *weights)
    return pl.pallas_call(
        functools.partial(project_kernel, head_count, len(pieces) // head_count),
        out_shape=jax.ShapeDtypeStruct((item_count, cols), jnp.bfloat16),
        in_specs=[pl.BlockSpec(memory_space=pltpu.SMEM)] + [vmem] * len(operands),
        out_specs=vmem,
        compiler_params=pltpu.CompilerParams(vmem_limit_bytes=16 << 20),
        cost_estimate=pl.CostEstimate(
            flops=2 * item_count * cols * cols * head_count,
            transcendentals=0,
            bytes_accessed=2 * cols * cols * head_count,
        ),
    )(scalars, *operands)


def head_split(catalog, cand_owner, cand_row, hist_len, proj_weight, keys, values, out_weight):
    user_count, ctx_count = lax.axis_size("user"), lax.axis_size("ctx")
    head_count = lax.axis_size("head")
    user, ctx, head = (lax.axis_index(a) for a in ("user", "ctx", "head"))
    shard_rows, model_width = catalog.shape
    col_share = proj_weight.shape[2]
    width = col_share // ctx_count
    cand_count = cand_row.shape[1]
    slot_count = ctx_count * (2 * cand_count // user_count)
    key_rows, value_rows = keys[0], values[0]
    scalars = jnp.stack([hist_len[0], user, ctx]).astype(jnp.int32)

    ids = cand_owner[0].reshape(1, cand_count) * shard_rows + cand_row
    ids = jnp.concatenate([ids] + [swap(ids, "ctx", k) for k in range(1, ctx_count)], axis=1)
    step = 1
    while step < user_count:
        ids = jnp.concatenate([ids, swap(ids, "user", step)], axis=0)
        step *= 2

    key_parts, value_parts = [key_rows], [value_rows]
    for k in range(1, ctx_count):
        at = (ctx ^ k) * width
        key_parts.append(swap(lax.dynamic_slice_in_dim(key_rows, at, width, 1), "ctx", k))
        value_parts.append(swap(lax.dynamic_slice_in_dim(value_rows, at, width, 1), "ctx", k))

    rows = silu(
        jnp.dot(
            catalog,
            proj_weight.reshape(model_width, 2 * col_share),
            preferred_element_type=jnp.float32,
        )
    ).astype(jnp.bfloat16)
    slots, ranks, *served = serve(scalars, ids, rows, slot_count, width)
    fetched = {k: swap(served[k - 1], "user", k) for k in range(user_count - 1, 0, -1)}
    plan, query, *served = serve_rest(scalars, slots, ranks, rows, width)
    queries = [query] + [fetched[k] for k in range(1, user_count)]
    fetched = {k: swap(served[k], "user", k) for k in range(user_count - 1, 0, -1)}
    gates = [served[0]] + [fetched[k] for k in range(1, user_count)]

    weights = [lax.dynamic_slice_in_dim(out_weight, head * col_share, col_share, 1)]
    for j in range(1, head_count):
        part = lax.dynamic_slice_in_dim(out_weight, (head ^ j) * col_share, col_share, 1)
        weights.append(swap(part, "head", j))

    pieces = [[None] * ctx_count for _ in range(head_count)]
    for k in range(ctx_count - 1, -1, -1):
        attended = attend(scalars, plan, queries, key_parts, value_parts, k)
        gated = gate(plan, attended, gates, k)
        pieces[0][k] = swap(gated, "ctx", k) if k > 0 else gated
    for k in range(ctx_count):
        for j in range(head_count - 1, 0, -1):
            pieces[j][k] = swap(pieces[0][k], "head", j)
    ranked = project_out(scalars, [p for row in pieces for p in row], weights)
    return ranked.reshape(1, cand_count, col_share)


def whole_heads(mesh, proj_weight):
    sizes = [mesh.shape[a] for a in ("user", "ctx", "head")]
    heads = proj_weight.shape[2] // mesh.shape["head"] // HEAD
    return all(n & (n - 1) == 0 for n in sizes) and heads % mesh.shape["ctx"] == 0


def solution(mesh):
    def run(catalog, cand_owner, cand_row, hist_len, proj_weight, keys, values, out_weight):
        per_device = head_split if whole_heads(mesh, proj_weight) else event_split
        return jax.shard_map(
            per_device,
            mesh=mesh,
            in_specs=(
                P("user", None),
                P("user", "ctx", None),
                P("user", "ctx"),
                P("user"),
                P(None, None, "head"),
                P("user", "ctx", "head"),
                P("user", "ctx", "head"),
                P("head", None),
            ),
            out_specs=P("user", "ctx", "head"),
            check_vma=False,
        )(catalog, cand_owner, cand_row, hist_len, proj_weight, keys, values, out_weight)

    return run
```

```python
import functools

import jax
import jax.numpy as jnp
from jax import lax
from jax.experimental import pallas as pl
from jax.experimental.pallas import tpu as pltpu
from jax.sharding import PartitionSpec as P

HEAD = 128


def attend_block(query_rows, key_rows, value_rows, offset, length):
    row_total = query_rows.shape[0]
    key_total = key_rows.shape[0]
    head_count = query_rows.shape[1] // HEAD
    query_heads = query_rows.reshape(row_total, head_count, HEAD)
    key_heads = key_rows.reshape(key_total, head_count, HEAD)
    value_heads = value_rows.reshape(key_total, head_count, HEAD)
    scores = jnp.einsum(
        "rhc,nhc->rhn", query_heads, key_heads, preferred_element_type=jnp.float32
    ) * HEAD ** (-0.5)
    places = offset + jnp.arange(key_total, dtype=jnp.int32)
    weights = jnp.where(
        places[None, None, :] < length, jax.nn.silu(scores) / length.astype(jnp.float32), 0.0
    ).astype(jnp.bfloat16)
    mixed_rows = jnp.einsum(
        "rhn,nhc->rhc", weights, value_heads, preferred_element_type=jnp.float32
    )
    return mixed_rows.reshape(row_total, head_count * HEAD)


def event_split(catalog, cand_owner, cand_row, hist_len, proj_weight, keys, values, out_weight):
    user_count = lax.axis_size("user")
    owners = cand_owner[0, :, 0]
    wanted = cand_row[0]
    cand_count = wanted.shape[0]
    slot_count = 2 * cand_count // user_count
    model_width = catalog.shape[1]
    col_share = proj_weight.shape[2]
    owner_hot = (owners[:, None] == jnp.arange(user_count, dtype=jnp.int32)[None, :]).astype(
        jnp.int32
    )
    rank_in = jnp.sum(jnp.cumsum(owner_hot, axis=0) * owner_hot, axis=1) - 1
    places = owners * slot_count + rank_in
    request = (
        jnp.zeros((user_count * slot_count,), jnp.int32)
        .at[places]
        .set(wanted)
        .reshape(user_count, slot_count)
    )
    weight_flat = proj_weight.reshape(model_width, 2 * col_share)
    asked_ids = lax.all_to_all(request, "user", split_axis=0, concat_axis=0, tiled=True)
    picked = jax.nn.silu(
        jnp.dot(
            jnp.take(catalog, asked_ids.reshape(-1), axis=0),
            weight_flat,
            preferred_element_type=jnp.float32,
        )
    ).astype(jnp.bfloat16)
    served = picked.reshape(asked_ids.shape[0], asked_ids.shape[1], 2 * col_share)
    returned = lax.all_to_all(served, "user", split_axis=0, concat_axis=0, tiled=True)
    own_rows = jnp.take(returned.reshape(user_count * slot_count, 2 * col_share), places, axis=0)
    queries = own_rows[:, :col_share]
    gates = own_rows[:, col_share:]
    length = hist_len[0]
    key_rows = keys[0]
    value_rows = values[0]
    all_queries = lax.all_gather(queries, "ctx", axis=0, tiled=True)
    offset = lax.axis_index("ctx") * key_rows.shape[0]
    attended = lax.psum_scatter(
        attend_block(all_queries, key_rows, value_rows, offset, length),
        "ctx",
        scatter_dimension=0,
        tiled=True,
    )
    gated_rows = (attended * gates.astype(jnp.float32)).astype(jnp.bfloat16)
    partials = jnp.dot(gated_rows, out_weight, preferred_element_type=jnp.float32)
    ranked = lax.psum_scatter(partials, "head", scatter_dimension=1, tiled=True).astype(
        jnp.bfloat16
    )
    return ranked.reshape(1, cand_count, col_share)


def swap(x, axis, k):
    return lax.ppermute(x, axis, [(i, i ^ k) for i in range(lax.axis_size(axis))])


def silu(x):
    half = 0.5 * x
    return half + half * jnp.tanh(half)


KEY_BLOCK = 512
LANES = 128


def one_hot(condition):
    return jnp.where(condition, 1.0, 0.0).astype(jnp.bfloat16)


def serve_kernel(piece_count, user_count, slot_count, scalars, *refs):
    rows_ref, slots_ref, ranks_ref, *out_refs = refs[piece_count:]
    user, ctx = scalars[1], scalars[2]
    shard_rows = rows_ref.shape[0]
    width = out_refs[0].shape[1]
    ids = jnp.concatenate([ref[...] for ref in refs[:piece_count]], axis=0)
    item_count = ids.shape[1]
    served = ids - user * shard_rows
    mine = [one_hot((served >= 0) & (served < shard_rows))]
    for k in range(user_count):
        own = ids[0:1] - (user ^ k) * shard_rows
        mine.append(one_hot((own >= 0) & (own < shard_rows)))
    mine = jnp.concatenate(mine, axis=0)
    before = one_hot(
        lax.broadcasted_iota(jnp.int32, (LANES, LANES), 0)
        < lax.broadcasted_iota(jnp.int32, (LANES, LANES), 1)
    )
    ranks, seen = [], jnp.zeros((mine.shape[0], 1), jnp.float32)
    for start in range(0, item_count, LANES):
        chunk = mine[:, start : start + LANES]
        ranks.append(jnp.dot(chunk, before, preferred_element_type=jnp.float32) + seen)
        seen += jnp.sum(chunk.astype(jnp.float32), axis=1, keepdims=True)
    rank = jnp.concatenate(ranks, axis=1)
    asked = mine[user_count:].astype(jnp.float32)
    shard = lax.broadcasted_iota(jnp.int32, asked.shape, 0).astype(jnp.float32)
    ranks_ref[0:1] = jnp.sum(asked * rank[user_count:], axis=0, keepdims=True)
    ranks_ref[1:2] = jnp.sum(asked * shard, axis=0, keepdims=True)
    served = jnp.clip(served, 0, shard_rows - 1)
    slot = lax.broadcasted_iota(jnp.int32, (slot_count, item_count), 0).astype(jnp.float32)
    row = lax.broadcasted_iota(jnp.int32, (slot_count, shard_rows), 1)
    cols = pl.ds(pl.multiple_of(ctx * width, width), width)
    for k in range(user_count):
        place = jnp.where(mine[k : k + 1] > 0, rank[k : k + 1], -1.0)
        parts = jnp.concatenate([served[k : k + 1] >> 8, served[k : k + 1] & 255], axis=0)
        found = lax.dot_general(
            one_hot(slot == place),
            parts.astype(jnp.float32).astype(jnp.bfloat16),
            (((1,), (1,)), ((), ())),
            preferred_element_type=jnp.float32,
        )
        at = (found[:, 0:1] * 256.0 + found[:, 1:2]).astype(jnp.int32)
        slots_ref[:, k : k + 1] = at
        if k > 0:
            out_refs[k - 1][...] = jnp.dot(
                one_hot(row == at), rows_ref[:, cols], preferred_element_type=jnp.float32
            ).astype(jnp.bfloat16)


def serve(scalars, pieces, rows, slot_count, width):
    user_count, item_count = sum(p.shape[0] for p in pieces), pieces[0].shape[1]
    vmem = pl.BlockSpec(memory_space=pltpu.VMEM)
    return pl.pallas_call(
        functools.partial(serve_kernel, len(pieces), user_count, slot_count),
        out_shape=[
            jax.ShapeDtypeStruct((slot_count, user_count), jnp.int32),
            jax.ShapeDtypeStruct((2, item_count), jnp.float32),
        ]
        + [jax.ShapeDtypeStruct((slot_count, width), jnp.bfloat16)] * (user_count - 1),
        in_specs=[pl.BlockSpec(memory_space=pltpu.SMEM)] + [vmem] * (len(pieces) + 1),
        out_specs=[vmem] * (user_count + 1),
        compiler_params=pltpu.CompilerParams(vmem_limit_bytes=16 << 20),
        cost_estimate=pl.CostEstimate(
            flops=2 * user_count * slot_count * rows.shape[0] * width,
            transcendentals=0,
            bytes_accessed=2 * rows.shape[0] * width,
        ),
    )(scalars, *pieces, rows)


def serve_rest_kernel(user_count, scalars, slots_ref, ranks_ref, rows_ref, plan_ref, query_ref, *out_refs):
    ctx = scalars[2]
    shard_rows, both = rows_ref.shape
    slot_count, width = query_ref.shape
    query_cols = pl.ds(pl.multiple_of(ctx * width, width), width)
    gate_slots = out_refs[0].shape[0]
    row = lax.broadcasted_iota(jnp.int32, (slot_count, shard_rows), 1)
    for k in range(user_count):
        hot = one_hot(row == slots_ref[:, k : k + 1])
        out_refs[k][...] = jnp.dot(
            hot[:gate_slots], rows_ref[:, both // 2 :], preferred_element_type=jnp.float32
        ).astype(jnp.bfloat16)
        if k == 0:
            query_ref[...] = jnp.dot(
                hot, rows_ref[:, query_cols], preferred_element_type=jnp.float32
            ).astype(jnp.bfloat16)
    item_count = ranks_ref.shape[1]
    same = one_hot(
        lax.broadcasted_iota(jnp.int32, (item_count, item_count), 0)
        == lax.broadcasted_iota(jnp.int32, (item_count, item_count), 1)
    )
    found = lax.dot_general(
        same,
        ranks_ref[...].astype(jnp.bfloat16),
        (((1,), (1,)), ((), ())),
        preferred_element_type=jnp.float32,
    )
    plan_ref[...] = (found[:, 0:1] + found[:, 1:2] * slot_count).astype(jnp.int32)


def serve_rest(scalars, slots, ranks, rows, width):
    slot_count, user_count = slots.shape
    both = rows.shape[1]
    vmem = pl.BlockSpec(memory_space=pltpu.VMEM)
    return pl.pallas_call(
        functools.partial(serve_rest_kernel, user_count),
        out_shape=[
            jax.ShapeDtypeStruct((ranks.shape[1], 1), jnp.int32),
            jax.ShapeDtypeStruct((slot_count, width), jnp.bfloat16),
        ]
        + [jax.ShapeDtypeStruct((slot_count * width * 2 // both, both // 2), jnp.bfloat16)]
        * user_count,
        in_specs=[pl.BlockSpec(memory_space=pltpu.SMEM), vmem, vmem, vmem],
        out_specs=[vmem] * (user_count + 2),
        compiler_params=pltpu.CompilerParams(vmem_limit_bytes=16 << 20),
        cost_estimate=pl.CostEstimate(
            flops=2 * user_count * slot_count * rows.shape[0] * width,
            transcendentals=0,
            bytes_accessed=2 * rows.shape[0] * width,
        ),
    )(scalars, slots, ranks, rows)


def pick(plan, stride, slot_rows):
    slot_count, width = slot_rows[0].shape
    slot = lax.broadcasted_iota(jnp.int32, (plan.shape[0], slot_count), 1)
    total = jnp.zeros((plan.shape[0], width), jnp.float32)
    for k, rows in enumerate(slot_rows):
        total += jnp.dot(
            one_hot(slot == plan - k * stride), rows, preferred_element_type=jnp.float32
        )
    return total


def attention_kernel(group, user_count, ctx_count, scalars, plan_ref, *refs):
    query_refs = refs[:user_count]
    key_refs = refs[user_count : user_count + ctx_count]
    value_refs = refs[user_count + ctx_count : user_count + 2 * ctx_count]
    out_ref = refs[-1]
    length, ctx = scalars[0], scalars[2]
    item_count, width = out_ref.shape
    plan = plan_ref[group * item_count : (group + 1) * item_count, :]
    stride = query_refs[0].shape[0]
    query = pick(plan, stride, [ref[...] for ref in query_refs]).astype(jnp.bfloat16)
    event_count = value_refs[0].shape[0]
    scale = 0.5 * HEAD ** (-0.5)
    scale_len = scale / jnp.full((1, 1), length, jnp.int32).astype(jnp.float32)
    for head in range(width // HEAD):
        cols = slice(head * HEAD, (head + 1) * HEAD)
        total = jnp.zeros((item_count, HEAD), jnp.float32)
        for k in range(ctx_count):
            first = (ctx ^ k) * event_count
            for start in range(0, event_count, KEY_BLOCK):
                rows = slice(start, start + KEY_BLOCK)
                if k == 0:
                    at = pl.ds(pl.multiple_of(ctx * width + head * HEAD, HEAD), HEAD)
                    key, value = key_refs[0][rows, at], value_refs[0][rows, at]
                else:
                    key, value = key_refs[k][rows, cols], value_refs[k][rows, cols]
                place = first + start + lax.broadcasted_iota(jnp.int32, value.shape, 0)
                value = jnp.where(place < length, value, jnp.zeros_like(value))
                raw = lax.dot_general(
                    query[:, cols],
                    key,
                    (((1,), (1,)), ((), ())),
                    preferred_element_type=jnp.float32,
                )
                lead = raw * scale_len
                weights = (lead + lead * jnp.tanh(raw * scale)).astype(jnp.bfloat16)
                total += jnp.dot(weights, value, preferred_element_type=jnp.float32)
        out_ref[:, cols] = total


def attend(scalars, plan, queries, key_parts, value_parts, group):
    slot_count, width = queries[0].shape
    user_count, ctx_count = len(queries), len(key_parts)
    item_count = plan.shape[0] // ctx_count
    events = ctx_count * value_parts[0].shape[0]
    vmem = pl.BlockSpec(memory_space=pltpu.VMEM)
    operands = (plan, *queries, *key_parts, *value_parts)
    return pl.pallas_call(
        functools.partial(attention_kernel, group, user_count, ctx_count),
        out_shape=jax.ShapeDtypeStruct((item_count, width), jnp.float32),
        in_specs=[pl.BlockSpec(memory_space=pltpu.SMEM)] + [vmem] * len(operands),
        out_specs=vmem,
        compiler_params=pltpu.CompilerParams(vmem_limit_bytes=24 << 20),
        cost_estimate=pl.CostEstimate(
            flops=4 * item_count * events * width,
            transcendentals=item_count * events * (width // HEAD),
            bytes_accessed=4 * events * width,
        ),
    )(scalars, *operands)


def gate_kernel(part, stride, scalars, plan_ref, attended_ref, *refs):
    gate_refs, out_ref = refs[:-1], refs[-1]
    item_count, width = out_ref.shape
    cols = pl.ds(pl.multiple_of((scalars[2] ^ part) * width, width), width)
    gates = pick(plan_ref[:item_count, :], stride, [ref[:, cols] for ref in gate_refs])
    out_ref[...] = (attended_ref[...] * gates).astype(out_ref.dtype)


def gate(scalars, plan, attended, gates, part, stride):
    vmem = pl.BlockSpec(memory_space=pltpu.VMEM)
    operands = (plan, attended, *gates)
    return pl.pallas_call(
        functools.partial(gate_kernel, part, stride),
        out_shape=jax.ShapeDtypeStruct(attended.shape, jnp.bfloat16),
        in_specs=[pl.BlockSpec(memory_space=pltpu.SMEM)] + [vmem] * len(operands),
        out_specs=vmem,
        compiler_params=pltpu.CompilerParams(vmem_limit_bytes=16 << 20),
        cost_estimate=pl.CostEstimate(
            flops=2 * attended.size * len(gates) * gates[0].shape[0],
            transcendentals=0,
            bytes_accessed=6 * attended.size,
        ),
    )(scalars, *operands)


def project_kernel(head_count, part, scalars, *refs):
    pieces, weights = refs[:head_count], refs[head_count : 2 * head_count]
    out_ref = refs[-1]
    width = pieces[0].shape[1]
    rows = pl.ds(pl.multiple_of((scalars[2] ^ part) * width, width), width)
    total = jnp.zeros(out_ref.shape, jnp.float32)
    if len(refs) > 2 * head_count + 1:
        total = refs[2 * head_count][...]
    for piece, weight in zip(pieces, weights, strict=True):
        total += jnp.dot(piece[...], weight[rows, :], preferred_element_type=jnp.float32)
    out_ref[...] = total.astype(out_ref.dtype)


def project_out(scalars, pieces, weights, part, before, dtype):
    item_count, width = pieces[0].shape
    cols = weights[0].shape[1]
    vmem = pl.BlockSpec(memory_space=pltpu.VMEM)
    operands = (*pieces, *weights) + (() if before is None else (before,))
    return pl.pallas_call(
        functools.partial(project_kernel, len(pieces), part),
        out_shape=jax.ShapeDtypeStruct((item_count, cols), dtype),
        in_specs=[pl.BlockSpec(memory_space=pltpu.SMEM)] + [vmem] * len(operands),
        out_specs=vmem,
        compiler_params=pltpu.CompilerParams(vmem_limit_bytes=16 << 20),
        cost_estimate=pl.CostEstimate(
            flops=2 * item_count * cols * width * len(pieces),
            transcendentals=0,
            bytes_accessed=2 * cols * width * len(pieces),
        ),
    )(scalars, *operands)


def after(x, *others):
    return lax.optimization_barrier((x, *others))[0]


def head_split(catalog, cand_owner, cand_row, hist_len, proj_weight, keys, values, out_weight):
    user_count, ctx_count = lax.axis_size("user"), lax.axis_size("ctx")
    head_count = lax.axis_size("head")
    user, ctx, head = (lax.axis_index(a) for a in ("user", "ctx", "head"))
    shard_rows, model_width = catalog.shape
    col_share = proj_weight.shape[2]
    width = col_share // ctx_count
    cand_count = cand_row.shape[1]
    slot_count = ctx_count * (2 * cand_count // user_count)
    key_rows, value_rows = keys[0], values[0]
    scalars = jnp.stack([hist_len[0], user, ctx]).astype(jnp.int32)

    ids = cand_owner[0].reshape(1, cand_count) * shard_rows + cand_row
    ids = jnp.concatenate([ids] + [swap(ids, "ctx", k) for k in range(1, ctx_count)], axis=1)
    pieces, step = [ids], 1
    while step < user_count:
        pieces.append(swap(jnp.concatenate(pieces, axis=0), "user", step))
        step *= 2

    key_parts, value_parts = [key_rows], [value_rows]
    late_values = after(value_rows, ids)
    for k in range(1, ctx_count):
        at = (ctx ^ k) * width
        key_parts.append(swap(lax.dynamic_slice_in_dim(key_rows, at, width, 1), "ctx", k))
        value_parts.append(swap(lax.dynamic_slice_in_dim(late_values, at, width, 1), "ctx", k))

    rows = silu(
        jnp.dot(
            catalog,
            after(proj_weight, *pieces[:-1]).reshape(model_width, 2 * col_share),
            preferred_element_type=jnp.float32,
        )
    ).astype(jnp.bfloat16)
    slots, ranks, *served = serve(scalars, pieces, rows, slot_count, width)
    fetched = {k: swap(served[k - 1], "user", k) for k in range(user_count - 1, 0, -1)}
    plan, query, *served = serve_rest(scalars, slots, ranks, rows, width)
    queries = [query] + [fetched[k] for k in range(1, user_count)]
    fetched = {k: swap(served[k], "user", k) for k in range(user_count - 1, 0, -1)}
    gates = [served[0]] + [fetched[k] for k in range(1, user_count)]

    attended = [None] * ctx_count
    for k in range(ctx_count - 1, -1, -1):
        own = attend(scalars, plan, queries, key_parts, value_parts, k)
        attended[k] = swap(own, "ctx", k) if k > 0 else own
        if k == ctx_count - 1:
            late_weight = after(out_weight, own)

    weights = [lax.dynamic_slice_in_dim(late_weight, head * col_share, col_share, 1)]
    for j in range(1, head_count):
        part = lax.dynamic_slice_in_dim(late_weight, (head ^ j) * col_share, col_share, 1)
        weights.append(swap(part, "head", j))

    ranked = None
    for k in range(ctx_count):
        gated = gate(scalars, plan, attended[k], gates, k, slot_count)
        fetched = {j: swap(gated, "head", j) for j in range(head_count - 1, 0, -1)}
        parts = [gated] + [fetched[j] for j in range(1, head_count)]
        dtype = jnp.bfloat16 if k == ctx_count - 1 else jnp.float32
        ranked = project_out(scalars, parts, weights, k, ranked, dtype)
    return ranked.reshape(1, cand_count, col_share)


def whole_heads(mesh, proj_weight):
    sizes = [mesh.shape[a] for a in ("user", "ctx", "head")]
    heads = proj_weight.shape[2] // mesh.shape["head"] // HEAD
    return all(n & (n - 1) == 0 for n in sizes) and heads % mesh.shape["ctx"] == 0


def solution(mesh):
    def run(catalog, cand_owner, cand_row, hist_len, proj_weight, keys, values, out_weight):
        per_device = head_split if whole_heads(mesh, proj_weight) else event_split
        return jax.shard_map(
            per_device,
            mesh=mesh,
            in_specs=(
                P("user", None),
                P("user", "ctx", None),
                P("user", "ctx"),
                P("user"),
                P(None, None, "head"),
                P("user", "ctx", "head"),
                P("user", "ctx", "head"),
                P("head", None),
            ),
            out_specs=P("user", "ctx", "head"),
            check_vma=False,
        )(catalog, cand_owner, cand_row, hist_len, proj_weight, keys, values, out_weight)

    return run
```

```python
import functools

import jax
import jax.numpy as jnp
from jax import lax
from jax.experimental import pallas as pl
from jax.experimental.pallas import tpu as pltpu
from jax.sharding import PartitionSpec as P


HEAD = 128


def attend_block(query_rows, key_rows, value_rows, offset, length):
    row_total = query_rows.shape[0]
    key_total = key_rows.shape[0]
    head_count = query_rows.shape[1] // HEAD
    query_heads = query_rows.reshape(row_total, head_count, HEAD)
    key_heads = key_rows.reshape(key_total, head_count, HEAD)
    value_heads = value_rows.reshape(key_total, head_count, HEAD)
    scores = jnp.einsum(
        "rhc,nhc->rhn", query_heads, key_heads, preferred_element_type=jnp.float32
    ) * HEAD ** (-0.5)
    places = offset + jnp.arange(key_total, dtype=jnp.int32)
    weights = jnp.where(
        places[None, None, :] < length, jax.nn.silu(scores) / length.astype(jnp.float32), 0.0
    ).astype(jnp.bfloat16)
    mixed_rows = jnp.einsum(
        "rhn,nhc->rhc", weights, value_heads, preferred_element_type=jnp.float32
    )
    return mixed_rows.reshape(row_total, head_count * HEAD)


def event_split(catalog, cand_owner, cand_row, hist_len, proj_weight, keys, values, out_weight):
    user_count = lax.axis_size("user")
    owners = cand_owner[0, :, 0]
    wanted = cand_row[0]
    cand_count = wanted.shape[0]
    slot_count = 2 * cand_count // user_count
    model_width = catalog.shape[1]
    col_share = proj_weight.shape[2]
    owner_hot = (owners[:, None] == jnp.arange(user_count, dtype=jnp.int32)[None, :]).astype(
        jnp.int32
    )
    rank_in = jnp.sum(jnp.cumsum(owner_hot, axis=0) * owner_hot, axis=1) - 1
    places = owners * slot_count + rank_in
    request = (
        jnp.zeros((user_count * slot_count,), jnp.int32)
        .at[places]
        .set(wanted)
        .reshape(user_count, slot_count)
    )
    weight_flat = proj_weight.reshape(model_width, 2 * col_share)
    asked_ids = lax.all_to_all(request, "user", split_axis=0, concat_axis=0, tiled=True)
    picked = jax.nn.silu(
        jnp.dot(
            jnp.take(catalog, asked_ids.reshape(-1), axis=0),
            weight_flat,
            preferred_element_type=jnp.float32,
        )
    ).astype(jnp.bfloat16)
    served = picked.reshape(asked_ids.shape[0], asked_ids.shape[1], 2 * col_share)
    returned = lax.all_to_all(served, "user", split_axis=0, concat_axis=0, tiled=True)
    own_rows = jnp.take(returned.reshape(user_count * slot_count, 2 * col_share), places, axis=0)
    queries = own_rows[:, :col_share]
    gates = own_rows[:, col_share:]
    length = hist_len[0]
    key_rows = keys[0]
    value_rows = values[0]
    all_queries = lax.all_gather(queries, "ctx", axis=0, tiled=True)
    offset = lax.axis_index("ctx") * key_rows.shape[0]
    attended = lax.psum_scatter(
        attend_block(all_queries, key_rows, value_rows, offset, length),
        "ctx",
        scatter_dimension=0,
        tiled=True,
    )
    gated_rows = (attended * gates.astype(jnp.float32)).astype(jnp.bfloat16)
    partials = jnp.dot(gated_rows, out_weight, preferred_element_type=jnp.float32)
    ranked = lax.psum_scatter(partials, "head", scatter_dimension=1, tiled=True).astype(
        jnp.bfloat16
    )
    return ranked.reshape(1, cand_count, col_share)


def swap(x, axis, k):
    return lax.ppermute(x, axis, [(i, i ^ k) for i in range(lax.axis_size(axis))])


def silu(x):
    half = 0.5 * x
    return half + half * jnp.tanh(half)


KEY_BLOCK = 512


def one_hot(condition):
    return jnp.where(condition, 1.0, 0.0).astype(jnp.bfloat16)


def shard_kernel(scalars, catalog_ref, weight_ref, query_ref, gate_ref):
    col_share, width = gate_ref.shape[1], query_ref.shape[1]
    cols = pl.ds(pl.multiple_of(scalars[2] * width, width), width)
    rows = catalog_ref[...]
    query = jnp.dot(rows, weight_ref[:, cols], preferred_element_type=jnp.float32)
    query_ref[...] = silu(query).astype(query_ref.dtype)
    gates = jnp.dot(rows, weight_ref[:, col_share:], preferred_element_type=jnp.float32)
    gate_ref[...] = silu(gates).astype(gate_ref.dtype)


def project_shard(scalars, catalog, weight, width):
    shard_rows, model_width = catalog.shape
    col_share = weight.shape[1] // 2
    vmem = pl.BlockSpec(memory_space=pltpu.VMEM)
    return pl.pallas_call(
        shard_kernel,
        out_shape=[
            jax.ShapeDtypeStruct((shard_rows, width), jnp.bfloat16),
            jax.ShapeDtypeStruct((shard_rows, col_share), jnp.bfloat16),
        ],
        in_specs=[pl.BlockSpec(memory_space=pltpu.SMEM), vmem, vmem],
        out_specs=[vmem, vmem],
        compiler_params=pltpu.CompilerParams(vmem_limit_bytes=16 << 20),
        cost_estimate=pl.CostEstimate(
            flops=2 * shard_rows * model_width * (col_share + width),
            transcendentals=shard_rows * (col_share + width),
            bytes_accessed=2 * model_width * (shard_rows + 2 * col_share),
        ),
    )(scalars, catalog, weight)


def serve_kernel(user_count, ctx_count, piece_count, scalars, *refs):
    piece_refs = refs[:piece_count]
    other_refs = refs[piece_count : piece_count + ctx_count - 1]
    rows_ref, plan_ref, gate_plan_ref, *out_refs = refs[piece_count + ctx_count - 1 :]
    user = scalars[1]
    shard_rows = rows_ref.shape[0]
    slot_count = out_refs[0].shape[0]
    ids = jnp.concatenate([ref[...] for ref in piece_refs], axis=0)
    item_count = ids.shape[1]
    same = one_hot(
        lax.broadcasted_iota(jnp.int32, (item_count, item_count), 0)
        == lax.broadcasted_iota(jnp.int32, (item_count, item_count), 1)
    )

    def columns(*rows):
        parts = jnp.concatenate([row.astype(jnp.float32) for row in rows], axis=0)
        return lax.dot_general(
            same,
            parts.astype(jnp.bfloat16),
            (((1,), (1,)), ((), ())),
            preferred_element_type=jnp.float32,
        )

    def owned_by(rows, shard):
        within = rows - shard * shard_rows
        return within, (within >= 0) & (within < shard_rows)

    for group, ref in enumerate((piece_refs[0], *other_refs)):
        place = jnp.zeros((1, item_count), jnp.int32)
        for k in range(user_count):
            within, owned = owned_by(ref[...], user ^ k)
            place = jnp.where(owned, within + k * shard_rows, place)
        found = columns(place >> 8, place & 255)
        plan_ref[group * item_count : (group + 1) * item_count, :] = (
            found[:, 0:1] * 256.0 + found[:, 1:2]
        ).astype(jnp.int32)

    served, asked = owned_by(ids, user)
    mine = [one_hot(asked)]
    for k in range(user_count):
        mine.append(one_hot(owned_by(ids[0:1], user ^ k)[1]))
    mine = jnp.concatenate(mine, axis=0)
    before = one_hot(
        lax.broadcasted_iota(jnp.int32, (item_count, item_count), 0)
        < lax.broadcasted_iota(jnp.int32, (item_count, item_count), 1)
    )
    rank = jnp.dot(mine, before, preferred_element_type=jnp.float32)
    own = mine[user_count:].astype(jnp.float32)
    shard = lax.broadcasted_iota(jnp.int32, own.shape, 0).astype(jnp.float32)
    found = columns(
        jnp.sum(own * shard, axis=0, keepdims=True),
        jnp.sum(own * rank[user_count:], axis=0, keepdims=True),
    )
    gate_plan_ref[...] = (found[:, 0:1] * slot_count + found[:, 1:2]).astype(jnp.int32)

    served = jnp.clip(served, 0, shard_rows - 1)
    slot = lax.broadcasted_iota(jnp.int32, (slot_count, item_count), 0).astype(jnp.float32)
    row = lax.broadcasted_iota(jnp.int32, (slot_count, shard_rows), 1)
    for k in range(user_count):
        place = jnp.where(mine[k : k + 1] > 0, rank[k : k + 1], -1.0)
        parts = jnp.concatenate([served[k : k + 1] >> 8, served[k : k + 1] & 255], axis=0)
        found = lax.dot_general(
            one_hot(slot == place),
            parts.astype(jnp.float32).astype(jnp.bfloat16),
            (((1,), (1,)), ((), ())),
            preferred_element_type=jnp.float32,
        )
        at = (found[:, 0:1] * 256.0 + found[:, 1:2]).astype(jnp.int32)
        out_refs[k][...] = jnp.dot(
            one_hot(row == at), rows_ref[...], preferred_element_type=jnp.float32
        ).astype(jnp.bfloat16)


def serve(scalars, pieces, others, rows, slot_count):
    user_count, item_count = sum(p.shape[0] for p in pieces), pieces[0].shape[1]
    ctx_count = len(others) + 1
    shard_rows, col_share = rows.shape
    vmem = pl.BlockSpec(memory_space=pltpu.VMEM)
    operands = (*pieces, *others, rows)
    return pl.pallas_call(
        functools.partial(serve_kernel, user_count, ctx_count, len(pieces)),
        out_shape=[
            jax.ShapeDtypeStruct((ctx_count * item_count, 1), jnp.int32),
            jax.ShapeDtypeStruct((item_count, 1), jnp.int32),
        ]
        + [jax.ShapeDtypeStruct((slot_count, col_share), jnp.bfloat16)] * user_count,
        in_specs=[pl.BlockSpec(memory_space=pltpu.SMEM)] + [vmem] * len(operands),
        out_specs=[vmem] * (user_count + 2),
        compiler_params=pltpu.CompilerParams(vmem_limit_bytes=16 << 20),
        cost_estimate=pl.CostEstimate(
            flops=2 * user_count * slot_count * shard_rows * col_share,
            transcendentals=0,
            bytes_accessed=2 * shard_rows * col_share,
        ),
    )(scalars, *operands)


def pick(plan, stride, slot_rows):
    slot_count, width = slot_rows[0].shape
    slot = lax.broadcasted_iota(jnp.int32, (plan.shape[0], slot_count), 1)
    total = jnp.zeros((plan.shape[0], width), jnp.float32)
    for k, rows in enumerate(slot_rows):
        total += jnp.dot(
            one_hot(slot == plan - k * stride), rows, preferred_element_type=jnp.float32
        )
    return total


def attention_kernel(group, user_count, ctx_count, scalars, plan_ref, *refs):
    query_refs = refs[:user_count]
    key_refs = refs[user_count : user_count + ctx_count]
    value_refs = refs[user_count + ctx_count : user_count + 2 * ctx_count]
    out_ref = refs[-1]
    length, ctx = scalars[0], scalars[2]
    item_count, width = out_ref.shape
    plan = plan_ref[group * item_count : (group + 1) * item_count, :]
    stride = query_refs[0].shape[0]
    query = pick(plan, stride, [ref[...] for ref in query_refs]).astype(jnp.bfloat16)
    event_count = value_refs[0].shape[0]
    scale = 0.5 * HEAD ** (-0.5)
    scale_len = scale / jnp.full((1, 1), length, jnp.int32).astype(jnp.float32)
    for head in range(width // HEAD):
        cols = slice(head * HEAD, (head + 1) * HEAD)
        total = jnp.zeros((item_count, HEAD), jnp.float32)
        for k in range(ctx_count):
            first = (ctx ^ k) * event_count
            for start in range(0, event_count, KEY_BLOCK):
                rows = slice(start, start + KEY_BLOCK)
                if k == 0:
                    at = pl.ds(pl.multiple_of(ctx * width + head * HEAD, HEAD), HEAD)
                    key, value = key_refs[0][rows, at], value_refs[0][rows, at]
                else:
                    key, value = key_refs[k][rows, cols], value_refs[k][rows, cols]
                place = first + start + lax.broadcasted_iota(jnp.int32, value.shape, 0)
                value = jnp.where(place < length, value, jnp.zeros_like(value))
                raw = lax.dot_general(
                    query[:, cols],
                    key,
                    (((1,), (1,)), ((), ())),
                    preferred_element_type=jnp.float32,
                )
                lead = raw * scale_len
                weights = (lead + lead * jnp.tanh(raw * scale)).astype(jnp.bfloat16)
                total += jnp.dot(weights, value, preferred_element_type=jnp.float32)
        out_ref[:, cols] = total.astype(out_ref.dtype)


def attend(scalars, plan, queries, key_parts, value_parts, group, dtype):
    width = queries[0].shape[1]
    user_count, ctx_count = len(queries), len(key_parts)
    item_count = plan.shape[0] // ctx_count
    events = ctx_count * value_parts[0].shape[0]
    vmem = pl.BlockSpec(memory_space=pltpu.VMEM)
    operands = (plan, *queries, *key_parts, *value_parts)
    return pl.pallas_call(
        functools.partial(attention_kernel, group, user_count, ctx_count),
        out_shape=jax.ShapeDtypeStruct((item_count, width), dtype),
        in_specs=[pl.BlockSpec(memory_space=pltpu.SMEM)] + [vmem] * len(operands),
        out_specs=vmem,
        compiler_params=pltpu.CompilerParams(vmem_limit_bytes=24 << 20),
        cost_estimate=pl.CostEstimate(
            flops=4 * item_count * events * width,
            transcendentals=item_count * events * (width // HEAD),
            bytes_accessed=4 * events * width,
        ),
    )(scalars, *operands)


def gate_kernel(part, scalars, plan_ref, attended_ref, *refs):
    gate_refs, out_ref = refs[:-1], refs[-1]
    width = out_ref.shape[1]
    cols = pl.ds(pl.multiple_of((scalars[2] ^ part) * width, width), width)
    stride = gate_refs[0].shape[0]
    gates = pick(plan_ref[...], stride, [ref[:, cols] for ref in gate_refs])
    out_ref[...] = (attended_ref[...].astype(jnp.float32) * gates).astype(out_ref.dtype)


def gate(scalars, plan, attended, gates, part):
    vmem = pl.BlockSpec(memory_space=pltpu.VMEM)
    operands = (plan, attended, *gates)
    return pl.pallas_call(
        functools.partial(gate_kernel, part),
        out_shape=jax.ShapeDtypeStruct(attended.shape, jnp.bfloat16),
        in_specs=[pl.BlockSpec(memory_space=pltpu.SMEM)] + [vmem] * len(operands),
        out_specs=vmem,
        compiler_params=pltpu.CompilerParams(vmem_limit_bytes=16 << 20),
        cost_estimate=pl.CostEstimate(
            flops=2 * attended.size * len(gates) * gates[0].shape[0],
            transcendentals=0,
            bytes_accessed=6 * attended.size,
        ),
    )(scalars, *operands)


def project_kernel(head_count, part, scalars, *refs):
    pieces, weights = refs[:head_count], refs[head_count : 2 * head_count]
    out_ref = refs[-1]
    width = pieces[0].shape[1]
    rows = pl.ds(pl.multiple_of((scalars[2] ^ part) * width, width), width)
    total = jnp.zeros(out_ref.shape, jnp.float32)
    if len(refs) > 2 * head_count + 1:
        total = refs[2 * head_count][...]
    for piece, weight in zip(pieces, weights, strict=True):
        total += jnp.dot(piece[...], weight[rows, :], preferred_element_type=jnp.float32)
    out_ref[...] = total.astype(out_ref.dtype)


def project_out(scalars, pieces, weights, part, before, dtype):
    item_count, width = pieces[0].shape
    cols = weights[0].shape[1]
    vmem = pl.BlockSpec(memory_space=pltpu.VMEM)
    operands = (*pieces, *weights) + (() if before is None else (before,))
    return pl.pallas_call(
        functools.partial(project_kernel, len(pieces), part),
        out_shape=jax.ShapeDtypeStruct((item_count, cols), dtype),
        in_specs=[pl.BlockSpec(memory_space=pltpu.SMEM)] + [vmem] * len(operands),
        out_specs=vmem,
        compiler_params=pltpu.CompilerParams(vmem_limit_bytes=16 << 20),
        cost_estimate=pl.CostEstimate(
            flops=2 * item_count * cols * width * len(pieces),
            transcendentals=0,
            bytes_accessed=2 * cols * width * len(pieces),
        ),
    )(scalars, *operands)


def after(x, *others):
    return lax.optimization_barrier((x, *others))[0]


def head_split(catalog, cand_owner, cand_row, hist_len, proj_weight, keys, values, out_weight):
    user_count, ctx_count = lax.axis_size("user"), lax.axis_size("ctx")
    head_count = lax.axis_size("head")
    user, ctx, head = (lax.axis_index(a) for a in ("user", "ctx", "head"))
    shard_rows, model_width = catalog.shape
    col_share = proj_weight.shape[2]
    width = col_share // ctx_count
    cand_count = cand_row.shape[1]
    slot_count = 2 * cand_count // user_count
    key_rows, value_rows = keys[0], values[0]
    scalars = jnp.stack([hist_len[0], user, ctx]).astype(jnp.int32)

    ids = cand_owner[0].reshape(1, cand_count) * shard_rows + cand_row
    others = [swap(ids, "ctx", k) for k in range(1, ctx_count)]

    key_parts, value_parts = [key_rows], [value_rows]
    for k in range(1, ctx_count):
        at = (ctx ^ k) * width
        key_part = lax.dynamic_slice_in_dim(key_rows, at, width, 1)
        key_parts.append(swap(key_part, "ctx", k))
        value_part = lax.dynamic_slice_in_dim(value_rows, at, width, 1)
        value_parts.append(swap(value_part, "ctx", k))

    weight = proj_weight.reshape(model_width, 2 * col_share)
    query, gate_rows = project_shard(scalars, catalog, weight, width)
    fetched = {k: swap(query, "user", k) for k in range(user_count - 1, 0, -1)}
    queries = [query] + [fetched[k] for k in range(1, user_count)]

    pieces, step = [after(ids, query)], 1
    while step < user_count:
        pieces.append(swap(jnp.concatenate(pieces, axis=0), "user", step))
        step *= 2
    plan, gate_plan, *served = serve(scalars, pieces, others, gate_rows, slot_count)
    fetched = {k: swap(served[k], "user", k) for k in range(user_count - 1, 0, -1)}
    gates = [served[0]] + [fetched[k] for k in range(1, user_count)]

    attended, late_weight = [None] * ctx_count, out_weight
    for k in range(ctx_count - 1, 0, -1):
        own = attend(scalars, plan, queries, key_parts, value_parts, k, jnp.bfloat16)
        attended[k] = swap(own, "ctx", k)
        if k == ctx_count - 1:
            late_weight = after(out_weight, own)
    attended[0] = attend(scalars, plan, queries, key_parts, value_parts, 0, jnp.float32)

    weights = [lax.dynamic_slice_in_dim(late_weight, head * col_share, col_share, 1)]
    for j in range(1, head_count):
        part = lax.dynamic_slice_in_dim(late_weight, (head ^ j) * col_share, col_share, 1)
        weights.append(swap(part, "head", j))

    ranked = None
    for k in range(ctx_count):
        gated = gate(scalars, gate_plan, attended[k], gates, k)
        fetched = {j: swap(gated, "head", j) for j in range(head_count - 1, 0, -1)}
        parts = [gated] + [fetched[j] for j in range(1, head_count)]
        dtype = jnp.bfloat16 if k == ctx_count - 1 else jnp.float32
        ranked = project_out(scalars, parts, weights, k, ranked, dtype)
    return ranked.reshape(1, cand_count, col_share)


def whole_heads(mesh, proj_weight):
    sizes = [mesh.shape[a] for a in ("user", "ctx", "head")]
    heads = proj_weight.shape[2] // mesh.shape["head"] // HEAD
    return all(n & (n - 1) == 0 for n in sizes) and heads % mesh.shape["ctx"] == 0


def solution(mesh):
    def step(per_device):
        return jax.shard_map(
            per_device,
            mesh=mesh,
            in_specs=(
                P("user", None),
                P("user", "ctx", None),
                P("user", "ctx"),
                P("user"),
                P(None, None, "head"),
                P("user", "ctx", "head"),
                P("user", "ctx", "head"),
                P("head", None),
            ),
            out_specs=P("user", "ctx", "head"),
            check_vma=False,
        )

    def run(catalog, cand_owner, cand_row, hist_len, proj_weight, keys, values, out_weight):
        args = (catalog, cand_owner, cand_row, hist_len, proj_weight, keys, values, out_weight)
        if not whole_heads(mesh, proj_weight):
            return step(event_split)(*args)
        return step(head_split)(*args)

    return run
```

```python
import functools

import jax
import jax.numpy as jnp
from jax import lax
from jax.experimental import pallas as pl
from jax.experimental.pallas import tpu as pltpu
from jax.sharding import PartitionSpec as P


HEAD = 128


def attend_block(query_rows, key_rows, value_rows, offset, length):
    row_total = query_rows.shape[0]
    key_total = key_rows.shape[0]
    head_count = query_rows.shape[1] // HEAD
    query_heads = query_rows.reshape(row_total, head_count, HEAD)
    key_heads = key_rows.reshape(key_total, head_count, HEAD)
    value_heads = value_rows.reshape(key_total, head_count, HEAD)
    scores = jnp.einsum(
        "rhc,nhc->rhn", query_heads, key_heads, preferred_element_type=jnp.float32
    ) * HEAD ** (-0.5)
    places = offset + jnp.arange(key_total, dtype=jnp.int32)
    weights = jnp.where(
        places[None, None, :] < length, jax.nn.silu(scores) / length.astype(jnp.float32), 0.0
    ).astype(jnp.bfloat16)
    mixed_rows = jnp.einsum(
        "rhn,nhc->rhc", weights, value_heads, preferred_element_type=jnp.float32
    )
    return mixed_rows.reshape(row_total, head_count * HEAD)


def event_split(catalog, cand_owner, cand_row, hist_len, proj_weight, keys, values, out_weight):
    user_count = lax.axis_size("user")
    owners = cand_owner[0, :, 0]
    wanted = cand_row[0]
    cand_count = wanted.shape[0]
    slot_count = 2 * cand_count // user_count
    model_width = catalog.shape[1]
    col_share = proj_weight.shape[2]
    owner_hot = (owners[:, None] == jnp.arange(user_count, dtype=jnp.int32)[None, :]).astype(
        jnp.int32
    )
    rank_in = jnp.sum(jnp.cumsum(owner_hot, axis=0) * owner_hot, axis=1) - 1
    places = owners * slot_count + rank_in
    request = (
        jnp.zeros((user_count * slot_count,), jnp.int32)
        .at[places]
        .set(wanted)
        .reshape(user_count, slot_count)
    )
    weight_flat = proj_weight.reshape(model_width, 2 * col_share)
    asked_ids = lax.all_to_all(request, "user", split_axis=0, concat_axis=0, tiled=True)
    picked = jax.nn.silu(
        jnp.dot(
            jnp.take(catalog, asked_ids.reshape(-1), axis=0),
            weight_flat,
            preferred_element_type=jnp.float32,
        )
    ).astype(jnp.bfloat16)
    served = picked.reshape(asked_ids.shape[0], asked_ids.shape[1], 2 * col_share)
    returned = lax.all_to_all(served, "user", split_axis=0, concat_axis=0, tiled=True)
    own_rows = jnp.take(returned.reshape(user_count * slot_count, 2 * col_share), places, axis=0)
    queries = own_rows[:, :col_share]
    gates = own_rows[:, col_share:]
    length = hist_len[0]
    key_rows = keys[0]
    value_rows = values[0]
    all_queries = lax.all_gather(queries, "ctx", axis=0, tiled=True)
    offset = lax.axis_index("ctx") * key_rows.shape[0]
    attended = lax.psum_scatter(
        attend_block(all_queries, key_rows, value_rows, offset, length),
        "ctx",
        scatter_dimension=0,
        tiled=True,
    )
    gated_rows = (attended * gates.astype(jnp.float32)).astype(jnp.bfloat16)
    partials = jnp.dot(gated_rows, out_weight, preferred_element_type=jnp.float32)
    ranked = lax.psum_scatter(partials, "head", scatter_dimension=1, tiled=True).astype(
        jnp.bfloat16
    )
    return ranked.reshape(1, cand_count, col_share)


def swap(x, axis, k):
    return lax.ppermute(x, axis, [(i, i ^ k) for i in range(lax.axis_size(axis))])


def columns_of(x, start, count):
    return lax.dynamic_slice_in_dim(x, start, count, 1)


def silu(x):
    half = 0.5 * x
    return half + half * jnp.tanh(half)


KEY_BLOCK = 256


def one_hot(condition):
    return jnp.where(condition, 1.0, 0.0).astype(jnp.bfloat16)


def shard_kernel(catalog_ref, weight_ref, query_ref, gate_ref):
    col_share, width = gate_ref.shape[1], query_ref.shape[1]
    cols = pl.ds(pl.multiple_of(lax.axis_index("ctx") * width, width), width)
    rows = catalog_ref[...]
    query = jnp.dot(rows, weight_ref[:, cols], preferred_element_type=jnp.float32)
    query_ref[...] = silu(query).astype(query_ref.dtype)
    gates = jnp.dot(rows, weight_ref[:, col_share:], preferred_element_type=jnp.float32)
    gates = silu(gates).astype(gate_ref.dtype)
    for part in range(col_share // width):
        cols = pl.ds(pl.multiple_of((lax.axis_index("ctx") ^ part) * width, width), width)
        gate_ref[:, cols] = gates[:, part * width : (part + 1) * width]


def project_shard(catalog, weight, width):
    shard_rows, model_width = catalog.shape
    col_share = weight.shape[1] // 2
    vmem = pl.BlockSpec(memory_space=pltpu.VMEM)
    return pl.pallas_call(
        shard_kernel,
        out_shape=[
            jax.ShapeDtypeStruct((shard_rows, width), jnp.bfloat16),
            jax.ShapeDtypeStruct((shard_rows, col_share), jnp.bfloat16),
        ],
        in_specs=[vmem, vmem],
        out_specs=[vmem, vmem],
        compiler_params=pltpu.CompilerParams(vmem_limit_bytes=16 << 20),
        cost_estimate=pl.CostEstimate(
            flops=2 * shard_rows * model_width * (col_share + width),
            transcendentals=shard_rows * (col_share + width),
            bytes_accessed=2 * model_width * (shard_rows + 2 * col_share),
        ),
    )(catalog, weight)


def store_gates(ref, base, hot, gates_ref):
    width, col_share = ref.shape[1], gates_ref.shape[1]
    count = hot.shape[0] * width // col_share
    rows = jnp.dot(hot[:count], gates_ref[...], preferred_element_type=jnp.float32)
    rows = rows.astype(ref.dtype)
    for part in range(col_share // width):
        ref[base + part * count : base + (part + 1) * count, :] = rows[
            :, part * width : (part + 1) * width
        ]


def serve_kernel(piece_count, user_count, slot_count, *refs):
    rows_ref, gates_ref, slots_ref, ranks_ref, *out_refs = refs[piece_count:]
    user = lax.axis_index("user")
    shard_rows = rows_ref.shape[0]
    ids = jnp.concatenate([ref[...] for ref in refs[:piece_count]], axis=0)
    item_count = ids.shape[1]
    served = ids - user * shard_rows
    mine = [one_hot((served >= 0) & (served < shard_rows))]
    for k in range(user_count):
        own = ids[0:1] - (user ^ k) * shard_rows
        mine.append(one_hot((own >= 0) & (own < shard_rows)))
    mine = jnp.concatenate(mine, axis=0)
    before = one_hot(
        lax.broadcasted_iota(jnp.int32, (item_count, item_count), 0)
        < lax.broadcasted_iota(jnp.int32, (item_count, item_count), 1)
    )
    rank = jnp.dot(mine, before, preferred_element_type=jnp.float32)
    asked = mine[user_count:].astype(jnp.float32)
    shard = lax.broadcasted_iota(jnp.int32, asked.shape, 0).astype(jnp.float32)
    ranks_ref[0:1] = jnp.sum(asked * rank[user_count:], axis=0, keepdims=True)
    ranks_ref[1:2] = jnp.sum(asked * shard, axis=0, keepdims=True)
    served = jnp.clip(served, 0, shard_rows - 1)
    slot = lax.broadcasted_iota(jnp.int32, (slot_count, item_count), 0).astype(jnp.float32)
    row = lax.broadcasted_iota(jnp.int32, (slot_count, shard_rows), 1)
    for k in (*range(1, user_count), 0):
        place = jnp.where(mine[k : k + 1] > 0, rank[k : k + 1], -1.0)
        parts = jnp.concatenate([served[k : k + 1] >> 8, served[k : k + 1] & 255], axis=0)
        found = lax.dot_general(
            one_hot(slot == place),
            parts.astype(jnp.float32).astype(jnp.bfloat16),
            (((1,), (1,)), ((), ())),
            preferred_element_type=jnp.float32,
        )
        at = (found[:, 0:1] * 256.0 + found[:, 1:2]).astype(jnp.int32)
        slots_ref[:, k : k + 1] = at
        if k > 0:
            hot = one_hot(row == at)
            out_refs[k - 1][:slot_count, :] = jnp.dot(
                hot, rows_ref[...], preferred_element_type=jnp.float32
            ).astype(jnp.bfloat16)
        if k == 1:
            store_gates(out_refs[0], slot_count, hot, gates_ref)


def serve(pieces, rows, gates, slot_count, width):
    user_count, item_count = sum(p.shape[0] for p in pieces), pieces[0].shape[1]
    vmem = pl.BlockSpec(memory_space=pltpu.VMEM)
    return pl.pallas_call(
        functools.partial(serve_kernel, len(pieces), user_count, slot_count),
        out_shape=[
            jax.ShapeDtypeStruct((slot_count, user_count), jnp.int32),
            jax.ShapeDtypeStruct((2, item_count), jnp.float32),
        ]
        + [
            jax.ShapeDtypeStruct((slot_count * (2 if k == 1 else 1), width), jnp.bfloat16)
            for k in range(1, user_count)
        ],
        in_specs=[vmem] * (len(pieces) + 2),
        out_specs=[vmem] * (user_count + 1),
        compiler_params=pltpu.CompilerParams(vmem_limit_bytes=16 << 20),
        cost_estimate=pl.CostEstimate(
            flops=2 * user_count * slot_count * rows.shape[0] * width,
            transcendentals=0,
            bytes_accessed=2 * rows.shape[0] * width,
        ),
    )(*pieces, rows, gates)


def serve_rest_kernel(user_count, slots_ref, ranks_ref, rows_ref, gates_ref, plan_ref, query_ref, *out_refs):
    shard_rows = rows_ref.shape[0]
    slot_count = query_ref.shape[0]
    row = lax.broadcasted_iota(jnp.int32, (slot_count, shard_rows), 1)
    for ref, k in zip(out_refs, (0, *range(2, user_count)), strict=True):
        hot = one_hot(row == slots_ref[:, k : k + 1])
        store_gates(ref, 0, hot, gates_ref)
        if k == 0:
            query_ref[...] = jnp.dot(
                hot, rows_ref[...], preferred_element_type=jnp.float32
            ).astype(jnp.bfloat16)
    item_count = ranks_ref.shape[1]
    same = one_hot(
        lax.broadcasted_iota(jnp.int32, (item_count, item_count), 0)
        == lax.broadcasted_iota(jnp.int32, (item_count, item_count), 1)
    )
    found = lax.dot_general(
        same,
        ranks_ref[...].astype(jnp.bfloat16),
        (((1,), (1,)), ((), ())),
        preferred_element_type=jnp.float32,
    )
    plan_ref[...] = (found[:, 0:1] + found[:, 1:2] * slot_count).astype(jnp.int32)


def serve_rest(slots, ranks, rows, gates):
    slot_count, user_count = slots.shape
    (shard_rows, width), col_share = rows.shape, gates.shape[1]
    count = user_count - (user_count > 1)
    vmem = pl.BlockSpec(memory_space=pltpu.VMEM)
    return pl.pallas_call(
        functools.partial(serve_rest_kernel, user_count),
        out_shape=[jax.ShapeDtypeStruct((ranks.shape[1], 1), jnp.int32)]
        + [jax.ShapeDtypeStruct((slot_count, width), jnp.bfloat16)] * (count + 1),
        in_specs=[vmem] * 4,
        out_specs=[vmem] * (count + 2),
        compiler_params=pltpu.CompilerParams(vmem_limit_bytes=16 << 20),
        cost_estimate=pl.CostEstimate(
            flops=2 * count * slot_count * shard_rows * width,
            transcendentals=0,
            bytes_accessed=2 * shard_rows * col_share,
        ),
    )(slots, ranks, rows, gates)


def pick(plan, stride, slot_rows):
    slot_count, width = slot_rows[0].shape
    slot = lax.broadcasted_iota(jnp.int32, (plan.shape[0], slot_count), 1)
    total = jnp.zeros((plan.shape[0], width), jnp.float32)
    for k, rows in enumerate(slot_rows):
        total += jnp.dot(
            one_hot(slot == plan - k * stride), rows, preferred_element_type=jnp.float32
        )
    return total


def attention_kernel(group, user_count, length_ref, plan_ref, *refs):
    query_refs, out_ref = refs[:user_count], refs[-1]
    key_ref, value_ref, *event_refs = refs[user_count:-1]
    ctx, length = lax.axis_index("ctx"), length_ref[...]
    item_count, width = out_ref.shape
    plan = plan_ref[group * item_count : (group + 1) * item_count, :]
    stride = query_refs[0].shape[0]
    query = pick(plan, stride, [ref[:stride, :] for ref in query_refs]).astype(jnp.bfloat16)
    event_count = key_ref.shape[0]
    scale = 0.5 * HEAD ** (-0.5)
    scale_len = scale / length.astype(jnp.float32)
    for head in range(width // HEAD):
        cols = slice(head * HEAD, (head + 1) * HEAD)
        total = jnp.zeros((item_count, HEAD), jnp.float32)
        for k in range(len(event_refs) + 1):
            first = (ctx ^ k) * event_count
            for start in range(0, event_count, KEY_BLOCK):
                stop = min(start + KEY_BLOCK, event_count)
                if k == 0:
                    at = pl.ds(pl.multiple_of(ctx * width + head * HEAD, HEAD), HEAD)
                    key, value = key_ref[start:stop, at], value_ref[start:stop, at]
                else:
                    key = event_refs[k - 1][start:stop, cols]
                    value = event_refs[k - 1][event_count + start : event_count + stop, cols]
                place = first + start + lax.broadcasted_iota(jnp.int32, value.shape, 0)
                value = jnp.where(place < length, value, jnp.zeros_like(value))
                raw = lax.dot_general(
                    query[:, cols],
                    key,
                    (((1,), (1,)), ((), ())),
                    preferred_element_type=jnp.float32,
                )
                lead = raw * scale_len
                weights = (lead + lead * jnp.tanh(raw * scale)).astype(jnp.bfloat16)
                total += jnp.dot(weights, value, preferred_element_type=jnp.float32)
        out_ref[:, cols] = total


def attend(length, plan, queries, keys, values, events, group):
    width = queries[0].shape[1]
    item_count = plan.shape[0] // (len(events) + 1)
    event_count = (len(events) + 1) * keys.shape[0]
    vmem = pl.BlockSpec(memory_space=pltpu.VMEM)
    operands = (length, plan, *queries, keys, values, *events)
    return pl.pallas_call(
        functools.partial(attention_kernel, group, len(queries)),
        out_shape=jax.ShapeDtypeStruct((item_count, width), jnp.float32),
        in_specs=[vmem] * len(operands),
        out_specs=vmem,
        compiler_params=pltpu.CompilerParams(vmem_limit_bytes=24 << 20),
        cost_estimate=pl.CostEstimate(
            flops=4 * item_count * event_count * width,
            transcendentals=item_count * event_count * (width // HEAD),
            bytes_accessed=4 * event_count * width,
        ),
    )(*operands)


def gate_kernel(part, part_count, stride, plan_ref, attended_ref, *refs):
    gate_refs, out_ref = refs[:-1], refs[-1]
    item_count = out_ref.shape[0]
    count = stride // part_count
    starts = [ref.shape[0] - stride + part * count for ref in gate_refs]
    slots = [ref[at : at + count, :] for at, ref in zip(starts, gate_refs, strict=True)]
    gates = pick(plan_ref[:item_count, :], stride, slots)
    out_ref[...] = (attended_ref[...] * gates).astype(out_ref.dtype)


def gate(plan, attended, gates, part, part_count):
    stride = gates[0].shape[0]
    vmem = pl.BlockSpec(memory_space=pltpu.VMEM)
    operands = (plan, attended, *gates)
    return pl.pallas_call(
        functools.partial(gate_kernel, part, part_count, stride),
        out_shape=jax.ShapeDtypeStruct(attended.shape, jnp.bfloat16),
        in_specs=[vmem] * len(operands),
        out_specs=vmem,
        compiler_params=pltpu.CompilerParams(vmem_limit_bytes=16 << 20),
        cost_estimate=pl.CostEstimate(
            flops=2 * attended.size * len(gates) * gates[0].shape[0],
            transcendentals=0,
            bytes_accessed=6 * attended.size,
        ),
    )(*operands)


def project_kernel(head_count, part, *refs):
    pieces, weights = refs[:head_count], refs[head_count : 2 * head_count]
    out_ref = refs[-1]
    width = pieces[0].shape[1]
    wanted = lax.axis_index("ctx") ^ part
    chosen = []
    for ref in weights:
        weight = ref[:width, :]
        for other in range(1, ref.shape[0] // width):
            rows = slice(other * width, (other + 1) * width)
            weight = jnp.where(wanted == other, ref[rows, :], weight)
        chosen.append(weight)
    total = jnp.dot(
        jnp.concatenate([piece[...] for piece in pieces], axis=1),
        jnp.concatenate(chosen, axis=0),
        preferred_element_type=jnp.float32,
    )
    if len(refs) > 2 * head_count + 1:
        total += refs[2 * head_count][...]
    out_ref[...] = total.astype(out_ref.dtype)


def project_out(pieces, weights, part, before, dtype):
    item_count, width = pieces[0].shape
    cols = weights[0].shape[1]
    vmem = pl.BlockSpec(memory_space=pltpu.VMEM)
    operands = (*pieces, *weights) + (() if before is None else (before,))
    return pl.pallas_call(
        functools.partial(project_kernel, len(pieces), part),
        out_shape=jax.ShapeDtypeStruct((item_count, cols), dtype),
        in_specs=[vmem] * len(operands),
        out_specs=vmem,
        compiler_params=pltpu.CompilerParams(vmem_limit_bytes=16 << 20),
        cost_estimate=pl.CostEstimate(
            flops=2 * item_count * cols * width * len(pieces),
            transcendentals=0,
            bytes_accessed=2 * cols * width * len(pieces),
        ),
    )(*operands)


def head_split(catalog, cand_owner, cand_row, hist_len, proj_weight, keys, values, out_weight):
    user_count, ctx_count = lax.axis_size("user"), lax.axis_size("ctx")
    head_count = lax.axis_size("head")
    ctx, head = lax.axis_index("ctx"), lax.axis_index("head")
    shard_rows, model_width = catalog.shape
    col_share = proj_weight.shape[2]
    width = col_share // ctx_count
    cand_count = cand_row.shape[1]
    slot_count = ctx_count * (2 * cand_count // user_count)
    key_rows, value_rows = keys[0], values[0]
    length = hist_len.reshape(1, 1)

    ids = cand_owner[0].reshape(1, cand_count) * shard_rows + cand_row
    others = [swap(ids, "ctx", k) for k in range(1, ctx_count)]
    pieces, step = [jnp.concatenate([ids, *others], axis=1)], 1
    while step < user_count:
        pieces.append(swap(jnp.concatenate(pieces, axis=0), "user", step))
        step *= 2

    events = []
    for k in range(1, ctx_count):
        at = (ctx ^ k) * width
        halves = [lax.dynamic_slice_in_dim(x, at, width, 1) for x in (key_rows, value_rows)]
        part = jnp.concatenate(halves, axis=0)
        events.append(swap(part, "ctx", k))

    weight = proj_weight.reshape(model_width, 2 * col_share)
    rows, gate_rows = project_shard(catalog, weight, width)
    slots, ranks, *served = serve(pieces, rows, gate_rows, slot_count, width)
    order = range(user_count - 1, 0, -1)
    fetched = {k: swap(served[k - 1], "user", k) for k in order}
    plan, query, *served = serve_rest(slots, ranks, rows, gate_rows)
    queries = [query] + [fetched[k] for k in range(1, user_count)]
    fetched = {k: swap(served[k - 1], "user", k) for k in order if k > 1}
    gates = [served[0], *queries[1:2]] + [fetched[k] for k in range(2, user_count)]

    weights = [columns_of(out_weight, head * col_share, col_share)]
    for j in range(1, head_count):
        part = columns_of(out_weight, (head ^ j) * col_share, col_share)
        weights.append(swap(part, "head", j))

    attended = [None] * ctx_count
    for k in range(ctx_count - 1, -1, -1):
        own = attend(length, plan, queries, key_rows, value_rows, events, k)
        attended[k] = swap(own, "ctx", k) if k > 0 else own

    ranked = None
    for k in range(ctx_count):
        gated = gate(plan, attended[k], gates, k, ctx_count)
        parts, bit = {0: gated}, head_count // 2
        while bit:
            for j in list(parts):
                parts[j ^ bit] = swap(parts[j], "head", bit)
            bit //= 2
        dtype = jnp.bfloat16 if k == ctx_count - 1 else jnp.float32
        heads = range(head_count)
        ranked = project_out(
            [parts[j] for j in heads], [weights[j] for j in heads], k, ranked, dtype
        )
    return ranked.reshape(1, cand_count, col_share)


def whole_heads(mesh, proj_weight):
    sizes = [mesh.shape[a] for a in ("user", "ctx", "head")]
    heads = proj_weight.shape[2] // mesh.shape["head"] // HEAD
    return all(n & (n - 1) == 0 for n in sizes) and heads % mesh.shape["ctx"] == 0 and sizes[0] > 1


def solution(mesh):
    def step(per_device):
        return jax.shard_map(
            per_device,
            mesh=mesh,
            in_specs=(
                P("user", None),
                P("user", "ctx", None),
                P("user", "ctx"),
                P("user"),
                P(None, None, "head"),
                P("user", "ctx", "head"),
                P("user", "ctx", "head"),
                P("head", None),
            ),
            out_specs=P("user", "ctx", "head"),
            check_vma=False,
        )

    def run(catalog, cand_owner, cand_row, hist_len, proj_weight, keys, values, out_weight):
        args = (catalog, cand_owner, cand_row, hist_len, proj_weight, keys, values, out_weight)
        if not whole_heads(mesh, proj_weight):
            return step(event_split)(*args)
        return step(head_split)(*args)

    return run
```

```python
import functools

import jax
import jax.numpy as jnp
from jax import lax
from jax.experimental import pallas as pl
from jax.experimental.pallas import tpu as pltpu
from jax.sharding import PartitionSpec as P


HEAD = 128


def attend_block(query_rows, key_rows, value_rows, offset, length):
    row_total = query_rows.shape[0]
    key_total = key_rows.shape[0]
    head_count = query_rows.shape[1] // HEAD
    query_heads = query_rows.reshape(row_total, head_count, HEAD)
    key_heads = key_rows.reshape(key_total, head_count, HEAD)
    value_heads = value_rows.reshape(key_total, head_count, HEAD)
    scores = jnp.einsum(
        "rhc,nhc->rhn", query_heads, key_heads, preferred_element_type=jnp.float32
    ) * HEAD ** (-0.5)
    places = offset + jnp.arange(key_total, dtype=jnp.int32)
    weights = jnp.where(
        places[None, None, :] < length, jax.nn.silu(scores) / length.astype(jnp.float32), 0.0
    ).astype(jnp.bfloat16)
    mixed_rows = jnp.einsum(
        "rhn,nhc->rhc", weights, value_heads, preferred_element_type=jnp.float32
    )
    return mixed_rows.reshape(row_total, head_count * HEAD)


def event_split(catalog, cand_owner, cand_row, hist_len, proj_weight, keys, values, out_weight):
    user_count = lax.axis_size("user")
    owners = cand_owner[0, :, 0]
    wanted = cand_row[0]
    cand_count = wanted.shape[0]
    slot_count = 2 * cand_count // user_count
    model_width = catalog.shape[1]
    col_share = proj_weight.shape[2]
    owner_hot = (owners[:, None] == jnp.arange(user_count, dtype=jnp.int32)[None, :]).astype(
        jnp.int32
    )
    rank_in = jnp.sum(jnp.cumsum(owner_hot, axis=0) * owner_hot, axis=1) - 1
    places = owners * slot_count + rank_in
    request = (
        jnp.zeros((user_count * slot_count,), jnp.int32)
        .at[places]
        .set(wanted)
        .reshape(user_count, slot_count)
    )
    weight_flat = proj_weight.reshape(model_width, 2 * col_share)
    asked_ids = lax.all_to_all(request, "user", split_axis=0, concat_axis=0, tiled=True)
    picked = jax.nn.silu(
        jnp.dot(
            jnp.take(catalog, asked_ids.reshape(-1), axis=0),
            weight_flat,
            preferred_element_type=jnp.float32,
        )
    ).astype(jnp.bfloat16)
    served = picked.reshape(asked_ids.shape[0], asked_ids.shape[1], 2 * col_share)
    returned = lax.all_to_all(served, "user", split_axis=0, concat_axis=0, tiled=True)
    own_rows = jnp.take(returned.reshape(user_count * slot_count, 2 * col_share), places, axis=0)
    queries = own_rows[:, :col_share]
    gates = own_rows[:, col_share:]
    length = hist_len[0]
    key_rows = keys[0]
    value_rows = values[0]
    all_queries = lax.all_gather(queries, "ctx", axis=0, tiled=True)
    offset = lax.axis_index("ctx") * key_rows.shape[0]
    attended = lax.psum_scatter(
        attend_block(all_queries, key_rows, value_rows, offset, length),
        "ctx",
        scatter_dimension=0,
        tiled=True,
    )
    gated_rows = (attended * gates.astype(jnp.float32)).astype(jnp.bfloat16)
    partials = jnp.dot(gated_rows, out_weight, preferred_element_type=jnp.float32)
    ranked = lax.psum_scatter(partials, "head", scatter_dimension=1, tiled=True).astype(
        jnp.bfloat16
    )
    return ranked.reshape(1, cand_count, col_share)


def swap(x, axis, k):
    return lax.ppermute(x, axis, [(i, i ^ k) for i in range(lax.axis_size(axis))])


def columns_of(x, start, count):
    return lax.dynamic_slice_in_dim(x, start, count, 1)


def silu(x):
    half = 0.5 * x
    return half + half * jnp.tanh(half)


KEY_BLOCK = 256
SPLIT = 3


def one_hot(condition):
    return jnp.where(condition, 1.0, 0.0).astype(jnp.bfloat16)


def split_kernel(partner, key_ref, value_ref, part_ref, held, read, written):
    events, width = key_ref.shape[0], part_ref.shape[1]
    cols = pl.ds(pl.multiple_of((lax.axis_index("ctx") ^ partner) * width, width), width)
    step = pl.cdiv(events, SPLIT)
    reads, writes = [], []
    for half, ref in enumerate((key_ref, value_ref)):
        for start in range(0, events, step):
            rows = slice(start, min(start + step, events))
            to = slice(half * events + rows.start, half * events + rows.stop)
            n = len(reads)
            reads.append(pltpu.make_async_copy(ref.at[rows, cols], held.at[to, :], read.at[n]))
            writes.append(
                pltpu.make_async_copy(held.at[to, :], part_ref.at[to, :], written.at[n])
            )
    for copy in reads:
        copy.start()
    for before, copy in zip(reads, writes, strict=True):
        before.wait()
        copy.start()
    for copy in writes:
        copy.wait()


def split_events(key_rows, value_rows, width, partner):
    events = key_rows.shape[0]
    whole = pl.BlockSpec(memory_space=pl.ANY)
    copies = pltpu.SemaphoreType.DMA((2 * SPLIT,))
    return pl.pallas_call(
        functools.partial(split_kernel, partner),
        out_shape=jax.ShapeDtypeStruct((2 * events, width), key_rows.dtype),
        in_specs=[whole, whole],
        out_specs=whole,
        scratch_shapes=[pltpu.VMEM((2 * events, width), key_rows.dtype), copies, copies],
        compiler_params=pltpu.CompilerParams(vmem_limit_bytes=60 << 20),
        cost_estimate=pl.CostEstimate(
            flops=0, transcendentals=0, bytes_accessed=8 * events * width
        ),
    )(key_rows, value_rows)


def shard_kernel(catalog_ref, weight_ref, query_ref, gate_ref):
    col_share, width = gate_ref.shape[1], query_ref.shape[1]
    cols = pl.ds(pl.multiple_of(lax.axis_index("ctx") * width, width), width)
    rows = catalog_ref[...]
    query = jnp.dot(rows, weight_ref[:, cols], preferred_element_type=jnp.float32)
    query_ref[...] = silu(query).astype(query_ref.dtype)
    gates = jnp.dot(rows, weight_ref[:, col_share:], preferred_element_type=jnp.float32)
    gates = silu(gates).astype(gate_ref.dtype)
    for part in range(col_share // width):
        cols = pl.ds(pl.multiple_of((lax.axis_index("ctx") ^ part) * width, width), width)
        gate_ref[:, cols] = gates[:, part * width : (part + 1) * width]


def project_shard(catalog, weight, width):
    shard_rows, model_width = catalog.shape
    col_share = weight.shape[1] // 2
    vmem = pl.BlockSpec(memory_space=pltpu.VMEM)
    return pl.pallas_call(
        shard_kernel,
        out_shape=[
            jax.ShapeDtypeStruct((shard_rows, width), jnp.bfloat16),
            jax.ShapeDtypeStruct((shard_rows, col_share), jnp.bfloat16),
        ],
        in_specs=[vmem, vmem],
        out_specs=[vmem, vmem],
        compiler_params=pltpu.CompilerParams(vmem_limit_bytes=16 << 20),
        cost_estimate=pl.CostEstimate(
            flops=2 * shard_rows * model_width * (col_share + width),
            transcendentals=shard_rows * (col_share + width),
            bytes_accessed=2 * model_width * (shard_rows + 2 * col_share),
        ),
    )(catalog, weight)


def store_gates(ref, base, hot, gates_ref):
    width, col_share = ref.shape[1], gates_ref.shape[1]
    count = hot.shape[0] * width // col_share
    rows = jnp.dot(hot[:count], gates_ref[...], preferred_element_type=jnp.float32)
    rows = rows.astype(ref.dtype)
    for part in range(col_share // width):
        ref[base + part * count : base + (part + 1) * count, :] = rows[
            :, part * width : (part + 1) * width
        ]


def serve_kernel(piece_count, user_count, slot_count, *refs):
    rows_ref, gates_ref, slots_ref, ranks_ref, *out_refs = refs[piece_count:]
    user = lax.axis_index("user")
    shard_rows = rows_ref.shape[0]
    ids = jnp.concatenate([ref[...] for ref in refs[:piece_count]], axis=0)
    item_count = ids.shape[1]
    served = ids - user * shard_rows
    mine = [one_hot((served >= 0) & (served < shard_rows))]
    for k in range(user_count):
        own = ids[0:1] - (user ^ k) * shard_rows
        mine.append(one_hot((own >= 0) & (own < shard_rows)))
    mine = jnp.concatenate(mine, axis=0)
    before = one_hot(
        lax.broadcasted_iota(jnp.int32, (item_count, item_count), 0)
        < lax.broadcasted_iota(jnp.int32, (item_count, item_count), 1)
    )
    rank = jnp.dot(mine, before, preferred_element_type=jnp.float32)
    asked = mine[user_count:].astype(jnp.float32)
    shard = lax.broadcasted_iota(jnp.int32, asked.shape, 0).astype(jnp.float32)
    ranks_ref[0:1] = jnp.sum(asked * rank[user_count:], axis=0, keepdims=True)
    ranks_ref[1:2] = jnp.sum(asked * shard, axis=0, keepdims=True)
    served = jnp.clip(served, 0, shard_rows - 1)
    slot = lax.broadcasted_iota(jnp.int32, (slot_count, item_count), 0).astype(jnp.float32)
    row = lax.broadcasted_iota(jnp.int32, (slot_count, shard_rows), 1)
    for k in (*range(1, user_count), 0):
        place = jnp.where(mine[k : k + 1] > 0, rank[k : k + 1], -1.0)
        parts = jnp.concatenate([served[k : k + 1] >> 8, served[k : k + 1] & 255], axis=0)
        found = lax.dot_general(
            one_hot(slot == place),
            parts.astype(jnp.float32).astype(jnp.bfloat16),
            (((1,), (1,)), ((), ())),
            preferred_element_type=jnp.float32,
        )
        at = (found[:, 0:1] * 256.0 + found[:, 1:2]).astype(jnp.int32)
        slots_ref[:, k : k + 1] = at
        if k > 0:
            hot = one_hot(row == at)
            out_refs[k - 1][:slot_count, :] = jnp.dot(
                hot, rows_ref[...], preferred_element_type=jnp.float32
            ).astype(jnp.bfloat16)
        if k == 1:
            store_gates(out_refs[0], slot_count, hot, gates_ref)


def serve(pieces, rows, gates, slot_count, width):
    user_count, item_count = sum(p.shape[0] for p in pieces), pieces[0].shape[1]
    vmem = pl.BlockSpec(memory_space=pltpu.VMEM)
    return pl.pallas_call(
        functools.partial(serve_kernel, len(pieces), user_count, slot_count),
        out_shape=[
            jax.ShapeDtypeStruct((slot_count, user_count), jnp.int32),
            jax.ShapeDtypeStruct((2, item_count), jnp.float32),
        ]
        + [
            jax.ShapeDtypeStruct((slot_count * (2 if k == 1 else 1), width), jnp.bfloat16)
            for k in range(1, user_count)
        ],
        in_specs=[vmem] * (len(pieces) + 2),
        out_specs=[vmem] * (user_count + 1),
        compiler_params=pltpu.CompilerParams(vmem_limit_bytes=16 << 20),
        cost_estimate=pl.CostEstimate(
            flops=2 * user_count * slot_count * rows.shape[0] * width,
            transcendentals=0,
            bytes_accessed=2 * rows.shape[0] * width,
        ),
    )(*pieces, rows, gates)


def serve_rest_kernel(user_count, slots_ref, ranks_ref, rows_ref, gates_ref, plan_ref, query_ref, *out_refs):
    shard_rows = rows_ref.shape[0]
    slot_count = query_ref.shape[0]
    row = lax.broadcasted_iota(jnp.int32, (slot_count, shard_rows), 1)
    for ref, k in zip(out_refs, (0, *range(2, user_count)), strict=True):
        hot = one_hot(row == slots_ref[:, k : k + 1])
        store_gates(ref, 0, hot, gates_ref)
        if k == 0:
            query_ref[...] = jnp.dot(
                hot, rows_ref[...], preferred_element_type=jnp.float32
            ).astype(jnp.bfloat16)
    item_count = ranks_ref.shape[1]
    same = one_hot(
        lax.broadcasted_iota(jnp.int32, (item_count, item_count), 0)
        == lax.broadcasted_iota(jnp.int32, (item_count, item_count), 1)
    )
    found = lax.dot_general(
        same,
        ranks_ref[...].astype(jnp.bfloat16),
        (((1,), (1,)), ((), ())),
        preferred_element_type=jnp.float32,
    )
    plan_ref[...] = (found[:, 0:1] + found[:, 1:2] * slot_count).astype(jnp.int32)


def serve_rest(slots, ranks, rows, gates):
    slot_count, user_count = slots.shape
    (shard_rows, width), col_share = rows.shape, gates.shape[1]
    count = user_count - (user_count > 1)
    vmem = pl.BlockSpec(memory_space=pltpu.VMEM)
    return pl.pallas_call(
        functools.partial(serve_rest_kernel, user_count),
        out_shape=[jax.ShapeDtypeStruct((ranks.shape[1], 1), jnp.int32)]
        + [jax.ShapeDtypeStruct((slot_count, width), jnp.bfloat16)] * (count + 1),
        in_specs=[vmem] * 4,
        out_specs=[vmem] * (count + 2),
        compiler_params=pltpu.CompilerParams(vmem_limit_bytes=16 << 20),
        cost_estimate=pl.CostEstimate(
            flops=2 * count * slot_count * shard_rows * width,
            transcendentals=0,
            bytes_accessed=2 * shard_rows * col_share,
        ),
    )(slots, ranks, rows, gates)


def pick(plan, stride, slot_rows):
    slot_count, width = slot_rows[0].shape
    slot = lax.broadcasted_iota(jnp.int32, (plan.shape[0], slot_count), 1)
    total = jnp.zeros((plan.shape[0], width), jnp.float32)
    for k, rows in enumerate(slot_rows):
        total += jnp.dot(
            one_hot(slot == plan - k * stride), rows, preferred_element_type=jnp.float32
        )
    return total


def attention_kernel(group, user_count, length_ref, plan_ref, *refs):
    query_refs, out_ref = refs[:user_count], refs[-1]
    key_ref, value_ref, *event_refs = refs[user_count:-1]
    ctx, length = lax.axis_index("ctx"), length_ref[...]
    item_count, width = out_ref.shape
    plan = plan_ref[group * item_count : (group + 1) * item_count, :]
    stride = query_refs[0].shape[0]
    query = pick(plan, stride, [ref[:stride, :] for ref in query_refs]).astype(jnp.bfloat16)
    event_count = key_ref.shape[0]
    scale = 0.5 * HEAD ** (-0.5)
    scale_len = scale / length.astype(jnp.float32)
    for head in range(width // HEAD):
        cols = slice(head * HEAD, (head + 1) * HEAD)
        total = jnp.zeros((item_count, HEAD), jnp.float32)
        for k in range(len(event_refs) + 1):
            first = (ctx ^ k) * event_count
            for start in range(0, event_count, KEY_BLOCK):
                stop = min(start + KEY_BLOCK, event_count)
                if k == 0:
                    at = pl.ds(pl.multiple_of(ctx * width + head * HEAD, HEAD), HEAD)
                    key, value = key_ref[start:stop, at], value_ref[start:stop, at]
                else:
                    key = event_refs[k - 1][start:stop, cols]
                    value = event_refs[k - 1][event_count + start : event_count + stop, cols]
                place = first + start + lax.broadcasted_iota(jnp.int32, value.shape, 0)
                value = jnp.where(place < length, value, jnp.zeros_like(value))
                raw = lax.dot_general(
                    query[:, cols],
                    key,
                    (((1,), (1,)), ((), ())),
                    preferred_element_type=jnp.float32,
                )
                lead = raw * scale_len
                weights = (lead + lead * jnp.tanh(raw * scale)).astype(jnp.bfloat16)
                total += jnp.dot(weights, value, preferred_element_type=jnp.float32)
        out_ref[:, cols] = total


def attend(length, plan, queries, keys, values, events, group):
    width = queries[0].shape[1]
    item_count = plan.shape[0] // (len(events) + 1)
    event_count = (len(events) + 1) * keys.shape[0]
    vmem = pl.BlockSpec(memory_space=pltpu.VMEM)
    operands = (length, plan, *queries, keys, values, *events)
    return pl.pallas_call(
        functools.partial(attention_kernel, group, len(queries)),
        out_shape=jax.ShapeDtypeStruct((item_count, width), jnp.float32),
        in_specs=[vmem] * len(operands),
        out_specs=vmem,
        compiler_params=pltpu.CompilerParams(vmem_limit_bytes=24 << 20),
        cost_estimate=pl.CostEstimate(
            flops=4 * item_count * event_count * width,
            transcendentals=item_count * event_count * (width // HEAD),
            bytes_accessed=4 * event_count * width,
        ),
    )(*operands)


def gate_kernel(part, part_count, stride, plan_ref, attended_ref, *refs):
    gate_refs, out_ref = refs[:-1], refs[-1]
    item_count = out_ref.shape[0]
    count = stride // part_count
    starts = [ref.shape[0] - stride + part * count for ref in gate_refs]
    slots = [ref[at : at + count, :] for at, ref in zip(starts, gate_refs, strict=True)]
    gates = pick(plan_ref[:item_count, :], stride, slots)
    out_ref[...] = (attended_ref[...] * gates).astype(out_ref.dtype)


def gate(plan, attended, gates, part, part_count):
    stride = gates[0].shape[0]
    vmem = pl.BlockSpec(memory_space=pltpu.VMEM)
    operands = (plan, attended, *gates)
    return pl.pallas_call(
        functools.partial(gate_kernel, part, part_count, stride),
        out_shape=jax.ShapeDtypeStruct(attended.shape, jnp.bfloat16),
        in_specs=[vmem] * len(operands),
        out_specs=vmem,
        compiler_params=pltpu.CompilerParams(vmem_limit_bytes=16 << 20),
        cost_estimate=pl.CostEstimate(
            flops=2 * attended.size * len(gates) * gates[0].shape[0],
            transcendentals=0,
            bytes_accessed=6 * attended.size,
        ),
    )(*operands)


def project_kernel(head_count, part, *refs):
    pieces, weights = refs[:head_count], refs[head_count : 2 * head_count]
    out_ref = refs[-1]
    width = pieces[0].shape[1]
    wanted = lax.axis_index("ctx") ^ part
    chosen = []
    for ref in weights:
        weight = ref[:width, :]
        for other in range(1, ref.shape[0] // width):
            rows = slice(other * width, (other + 1) * width)
            weight = jnp.where(wanted == other, ref[rows, :], weight)
        chosen.append(weight)
    total = jnp.dot(
        jnp.concatenate([piece[...] for piece in pieces], axis=1),
        jnp.concatenate(chosen, axis=0),
        preferred_element_type=jnp.float32,
    )
    if len(refs) > 2 * head_count + 1:
        total += refs[2 * head_count][...]
    out_ref[...] = total.astype(out_ref.dtype)


def project_out(pieces, weights, part, before, dtype):
    item_count, width = pieces[0].shape
    cols = weights[0].shape[1]
    vmem = pl.BlockSpec(memory_space=pltpu.VMEM)
    operands = (*pieces, *weights) + (() if before is None else (before,))
    return pl.pallas_call(
        functools.partial(project_kernel, len(pieces), part),
        out_shape=jax.ShapeDtypeStruct((item_count, cols), dtype),
        in_specs=[vmem] * len(operands),
        out_specs=vmem,
        compiler_params=pltpu.CompilerParams(vmem_limit_bytes=16 << 20),
        cost_estimate=pl.CostEstimate(
            flops=2 * item_count * cols * width * len(pieces),
            transcendentals=0,
            bytes_accessed=2 * cols * width * len(pieces),
        ),
    )(*operands)


def head_split(catalog, cand_owner, cand_row, hist_len, proj_weight, keys, values, out_weight):
    user_count, ctx_count = lax.axis_size("user"), lax.axis_size("ctx")
    head_count = lax.axis_size("head")
    head = lax.axis_index("head")
    shard_rows, model_width = catalog.shape
    col_share = proj_weight.shape[2]
    width = col_share // ctx_count
    cand_count = cand_row.shape[1]
    slot_count = ctx_count * (2 * cand_count // user_count)
    key_rows, value_rows = keys[0], values[0]
    length = hist_len.reshape(1, 1)

    ids = cand_owner[0].reshape(1, cand_count) * shard_rows + cand_row
    others = [swap(ids, "ctx", k) for k in range(1, ctx_count)]
    pieces, step = [jnp.concatenate([ids, *others], axis=1)], 1
    while step < user_count:
        pieces.append(swap(jnp.concatenate(pieces, axis=0), "user", step))
        step *= 2

    events = []
    for k in range(1, ctx_count):
        part = split_events(key_rows, value_rows, width, k)
        events.append(swap(part, "ctx", k))

    weight = proj_weight.reshape(model_width, 2 * col_share)
    rows, gate_rows = project_shard(catalog, weight, width)
    slots, ranks, *served = serve(pieces, rows, gate_rows, slot_count, width)
    order = range(user_count - 1, 0, -1)
    fetched = {k: swap(served[k - 1], "user", k) for k in order}
    plan, query, *served = serve_rest(slots, ranks, rows, gate_rows)
    queries = [query] + [fetched[k] for k in range(1, user_count)]
    fetched = {k: swap(served[k - 1], "user", k) for k in order if k > 1}
    gates = [served[0], *queries[1:2]] + [fetched[k] for k in range(2, user_count)]

    weights = [columns_of(out_weight, head * col_share, col_share)]
    for j in range(1, head_count):
        part = columns_of(out_weight, (head ^ j) * col_share, col_share)
        weights.append(swap(part, "head", j))

    attended = [None] * ctx_count
    for k in range(ctx_count - 1, -1, -1):
        own = attend(length, plan, queries, key_rows, value_rows, events, k)
        attended[k] = swap(own, "ctx", k) if k > 0 else own

    ranked = None
    for k in range(ctx_count):
        gated = gate(plan, attended[k], gates, k, ctx_count)
        parts, bit = {0: gated}, head_count // 2
        while bit:
            for j in list(parts):
                parts[j ^ bit] = swap(parts[j], "head", bit)
            bit //= 2
        dtype = jnp.bfloat16 if k == ctx_count - 1 else jnp.float32
        heads = range(head_count)
        ranked = project_out(
            [parts[j] for j in heads], [weights[j] for j in heads], k, ranked, dtype
        )
    return ranked.reshape(1, cand_count, col_share)


def whole_heads(mesh, proj_weight):
    sizes = [mesh.shape[a] for a in ("user", "ctx", "head")]
    heads = proj_weight.shape[2] // mesh.shape["head"] // HEAD
    return all(n & (n - 1) == 0 for n in sizes) and heads % mesh.shape["ctx"] == 0 and sizes[0] > 1


def solution(mesh):
    def step(per_device):
        return jax.shard_map(
            per_device,
            mesh=mesh,
            in_specs=(
                P("user", None),
                P("user", "ctx", None),
                P("user", "ctx"),
                P("user"),
                P(None, None, "head"),
                P("user", "ctx", "head"),
                P("user", "ctx", "head"),
                P("head", None),
            ),
            out_specs=P("user", "ctx", "head"),
            check_vma=False,
        )

    def run(catalog, cand_owner, cand_row, hist_len, proj_weight, keys, values, out_weight):
        args = (catalog, cand_owner, cand_row, hist_len, proj_weight, keys, values, out_weight)
        if not whole_heads(mesh, proj_weight):
            return step(event_split)(*args)
        return step(head_split)(*args)

    return run
```

```python
import functools

import jax
import jax.numpy as jnp
from jax import lax
from jax.experimental import pallas as pl
from jax.experimental.pallas import tpu as pltpu
from jax.sharding import PartitionSpec as P


HEAD = 128


def attend_block(query_rows, key_rows, value_rows, offset, length):
    row_total = query_rows.shape[0]
    key_total = key_rows.shape[0]
    head_count = query_rows.shape[1] // HEAD
    query_heads = query_rows.reshape(row_total, head_count, HEAD)
    key_heads = key_rows.reshape(key_total, head_count, HEAD)
    value_heads = value_rows.reshape(key_total, head_count, HEAD)
    scores = jnp.einsum(
        "rhc,nhc->rhn", query_heads, key_heads, preferred_element_type=jnp.float32
    ) * HEAD ** (-0.5)
    places = offset + jnp.arange(key_total, dtype=jnp.int32)
    weights = jnp.where(
        places[None, None, :] < length, jax.nn.silu(scores) / length.astype(jnp.float32), 0.0
    ).astype(jnp.bfloat16)
    mixed_rows = jnp.einsum(
        "rhn,nhc->rhc", weights, value_heads, preferred_element_type=jnp.float32
    )
    return mixed_rows.reshape(row_total, head_count * HEAD)


def event_split(catalog, cand_owner, cand_row, hist_len, proj_weight, keys, values, out_weight):
    user_count = lax.axis_size("user")
    owners = cand_owner[0, :, 0]
    wanted = cand_row[0]
    cand_count = wanted.shape[0]
    slot_count = 2 * cand_count // user_count
    model_width = catalog.shape[1]
    col_share = proj_weight.shape[2]
    owner_hot = (owners[:, None] == jnp.arange(user_count, dtype=jnp.int32)[None, :]).astype(
        jnp.int32
    )
    rank_in = jnp.sum(jnp.cumsum(owner_hot, axis=0) * owner_hot, axis=1) - 1
    places = owners * slot_count + rank_in
    request = (
        jnp.zeros((user_count * slot_count,), jnp.int32)
        .at[places]
        .set(wanted)
        .reshape(user_count, slot_count)
    )
    weight_flat = proj_weight.reshape(model_width, 2 * col_share)
    asked_ids = lax.all_to_all(request, "user", split_axis=0, concat_axis=0, tiled=True)
    picked = jax.nn.silu(
        jnp.dot(
            jnp.take(catalog, asked_ids.reshape(-1), axis=0),
            weight_flat,
            preferred_element_type=jnp.float32,
        )
    ).astype(jnp.bfloat16)
    served = picked.reshape(asked_ids.shape[0], asked_ids.shape[1], 2 * col_share)
    returned = lax.all_to_all(served, "user", split_axis=0, concat_axis=0, tiled=True)
    own_rows = jnp.take(returned.reshape(user_count * slot_count, 2 * col_share), places, axis=0)
    queries = own_rows[:, :col_share]
    gates = own_rows[:, col_share:]
    length = hist_len[0]
    key_rows = keys[0]
    value_rows = values[0]
    all_queries = lax.all_gather(queries, "ctx", axis=0, tiled=True)
    offset = lax.axis_index("ctx") * key_rows.shape[0]
    attended = lax.psum_scatter(
        attend_block(all_queries, key_rows, value_rows, offset, length),
        "ctx",
        scatter_dimension=0,
        tiled=True,
    )
    gated_rows = (attended * gates.astype(jnp.float32)).astype(jnp.bfloat16)
    partials = jnp.dot(gated_rows, out_weight, preferred_element_type=jnp.float32)
    ranked = lax.psum_scatter(partials, "head", scatter_dimension=1, tiled=True).astype(
        jnp.bfloat16
    )
    return ranked.reshape(1, cand_count, col_share)


def swap(x, axis, k):
    return lax.ppermute(x, axis, [(i, i ^ k) for i in range(lax.axis_size(axis))])


def columns_of(x, start, count):
    return lax.dynamic_slice_in_dim(x, start, count, 1)


def silu(x):
    half = 0.5 * x
    return half + half * jnp.tanh(half)


KEY_BLOCK = 256
SPLIT = 3


def one_hot(condition):
    return jnp.where(condition, 1.0, 0.0).astype(jnp.bfloat16)


def split_kernel(partner, key_ref, value_ref, part_ref, held, read, written):
    events, width = key_ref.shape[0], part_ref.shape[1]
    cols = pl.ds(pl.multiple_of((lax.axis_index("ctx") ^ partner) * width, width), width)
    step = pl.cdiv(events, SPLIT)
    reads, writes = [], []
    for half, ref in enumerate((key_ref, value_ref)):
        for start in range(0, events, step):
            rows = slice(start, min(start + step, events))
            to = slice(half * events + rows.start, half * events + rows.stop)
            n = len(reads)
            reads.append(pltpu.make_async_copy(ref.at[rows, cols], held.at[to, :], read.at[n]))
            writes.append(
                pltpu.make_async_copy(held.at[to, :], part_ref.at[to, :], written.at[n])
            )
    for copy in reads:
        copy.start()
    for before, copy in zip(reads, writes, strict=True):
        before.wait()
        copy.start()
    for copy in writes:
        copy.wait()


def split_events(key_rows, value_rows, width, partner):
    events = key_rows.shape[0]
    whole = pl.BlockSpec(memory_space=pl.ANY)
    copies = pltpu.SemaphoreType.DMA((2 * SPLIT,))
    return pl.pallas_call(
        functools.partial(split_kernel, partner),
        out_shape=jax.ShapeDtypeStruct((2 * events, width), key_rows.dtype),
        in_specs=[whole, whole],
        out_specs=whole,
        scratch_shapes=[pltpu.VMEM((2 * events, width), key_rows.dtype), copies, copies],
        compiler_params=pltpu.CompilerParams(vmem_limit_bytes=60 << 20),
        cost_estimate=pl.CostEstimate(
            flops=0, transcendentals=0, bytes_accessed=8 * events * width
        ),
    )(key_rows, value_rows)


def shard_kernel(catalog_ref, weight_ref, query_ref, gate_ref):
    col_share, width = gate_ref.shape[1], query_ref.shape[1]
    cols = pl.ds(pl.multiple_of(lax.axis_index("ctx") * width, width), width)
    rows = catalog_ref[...]
    query = jnp.dot(rows, weight_ref[:, cols], preferred_element_type=jnp.float32)
    query_ref[...] = silu(query).astype(query_ref.dtype)
    gates = jnp.dot(rows, weight_ref[:, col_share:], preferred_element_type=jnp.float32)
    gates = silu(gates).astype(gate_ref.dtype)
    for part in range(col_share // width):
        cols = pl.ds(pl.multiple_of((lax.axis_index("ctx") ^ part) * width, width), width)
        gate_ref[:, cols] = gates[:, part * width : (part + 1) * width]


def project_shard(catalog, weight, width):
    shard_rows, model_width = catalog.shape
    col_share = weight.shape[1] // 2
    vmem = pl.BlockSpec(memory_space=pltpu.VMEM)
    return pl.pallas_call(
        shard_kernel,
        out_shape=[
            jax.ShapeDtypeStruct((shard_rows, width), jnp.bfloat16),
            jax.ShapeDtypeStruct((shard_rows, col_share), jnp.bfloat16),
        ],
        in_specs=[vmem, vmem],
        out_specs=[vmem, vmem],
        compiler_params=pltpu.CompilerParams(vmem_limit_bytes=16 << 20),
        cost_estimate=pl.CostEstimate(
            flops=2 * shard_rows * model_width * (col_share + width),
            transcendentals=shard_rows * (col_share + width),
            bytes_accessed=2 * model_width * (shard_rows + 2 * col_share),
        ),
    )(catalog, weight)


def store_gates(ref, base, hot, gates_ref):
    width, col_share = ref.shape[1], gates_ref.shape[1]
    count = hot.shape[0] * width // col_share
    rows = jnp.dot(hot[:count], gates_ref[...], preferred_element_type=jnp.float32)
    rows = rows.astype(ref.dtype)
    for part in range(col_share // width):
        ref[base + part * count : base + (part + 1) * count, :] = rows[
            :, part * width : (part + 1) * width
        ]


def serve_kernel(piece_count, user_count, slot_count, *refs):
    rows_ref, gates_ref, slots_ref, ranks_ref, *out_refs = refs[piece_count:]
    user = lax.axis_index("user")
    shard_rows = rows_ref.shape[0]
    ids = jnp.concatenate([ref[...] for ref in refs[:piece_count]], axis=0)
    item_count = ids.shape[1]
    served = ids - user * shard_rows
    mine = [one_hot((served >= 0) & (served < shard_rows))]
    for k in range(user_count):
        own = ids[0:1] - (user ^ k) * shard_rows
        mine.append(one_hot((own >= 0) & (own < shard_rows)))
    mine = jnp.concatenate(mine, axis=0)
    before = one_hot(
        lax.broadcasted_iota(jnp.int32, (item_count, item_count), 0)
        < lax.broadcasted_iota(jnp.int32, (item_count, item_count), 1)
    )
    rank = jnp.dot(mine, before, preferred_element_type=jnp.float32)
    asked = mine[user_count:].astype(jnp.float32)
    shard = lax.broadcasted_iota(jnp.int32, asked.shape, 0).astype(jnp.float32)
    ranks_ref[0:1] = jnp.sum(asked * rank[user_count:], axis=0, keepdims=True)
    ranks_ref[1:2] = jnp.sum(asked * shard, axis=0, keepdims=True)
    served = jnp.clip(served, 0, shard_rows - 1)
    slot = lax.broadcasted_iota(jnp.int32, (slot_count, item_count), 0).astype(jnp.float32)
    row = lax.broadcasted_iota(jnp.int32, (slot_count, shard_rows), 1)
    for k in (*range(1, user_count), 0):
        place = jnp.where(mine[k : k + 1] > 0, rank[k : k + 1], -1.0)
        parts = jnp.concatenate([served[k : k + 1] >> 8, served[k : k + 1] & 255], axis=0)
        found = lax.dot_general(
            one_hot(slot == place),
            parts.astype(jnp.float32).astype(jnp.bfloat16),
            (((1,), (1,)), ((), ())),
            preferred_element_type=jnp.float32,
        )
        at = (found[:, 0:1] * 256.0 + found[:, 1:2]).astype(jnp.int32)
        slots_ref[:, k : k + 1] = at
        if k > 0:
            hot = one_hot(row == at)
            out_refs[k - 1][:slot_count, :] = jnp.dot(
                hot, rows_ref[...], preferred_element_type=jnp.float32
            ).astype(jnp.bfloat16)
        if k == 1:
            store_gates(out_refs[0], slot_count, hot, gates_ref)


def serve(pieces, rows, gates, slot_count, width):
    user_count, item_count = sum(p.shape[0] for p in pieces), pieces[0].shape[1]
    vmem = pl.BlockSpec(memory_space=pltpu.VMEM)
    return pl.pallas_call(
        functools.partial(serve_kernel, len(pieces), user_count, slot_count),
        out_shape=[
            jax.ShapeDtypeStruct((slot_count, user_count), jnp.int32),
            jax.ShapeDtypeStruct((2, item_count), jnp.float32),
        ]
        + [
            jax.ShapeDtypeStruct((slot_count * (2 if k == 1 else 1), width), jnp.bfloat16)
            for k in range(1, user_count)
        ],
        in_specs=[vmem] * (len(pieces) + 2),
        out_specs=[vmem] * (user_count + 1),
        compiler_params=pltpu.CompilerParams(vmem_limit_bytes=16 << 20),
        cost_estimate=pl.CostEstimate(
            flops=2 * user_count * slot_count * rows.shape[0] * width,
            transcendentals=0,
            bytes_accessed=2 * rows.shape[0] * width,
        ),
    )(*pieces, rows, gates)


def serve_rest_kernel(user_count, slots_ref, ranks_ref, rows_ref, gates_ref, plan_ref, query_ref, *out_refs):
    shard_rows = rows_ref.shape[0]
    slot_count = query_ref.shape[0]
    row = lax.broadcasted_iota(jnp.int32, (slot_count, shard_rows), 1)
    for ref, k in zip(out_refs, (0, *range(2, user_count)), strict=True):
        hot = one_hot(row == slots_ref[:, k : k + 1])
        store_gates(ref, 0, hot, gates_ref)
        if k == 0:
            query_ref[...] = jnp.dot(
                hot, rows_ref[...], preferred_element_type=jnp.float32
            ).astype(jnp.bfloat16)
    item_count = ranks_ref.shape[1]
    same = one_hot(
        lax.broadcasted_iota(jnp.int32, (item_count, item_count), 0)
        == lax.broadcasted_iota(jnp.int32, (item_count, item_count), 1)
    )
    found = lax.dot_general(
        same,
        ranks_ref[...].astype(jnp.bfloat16),
        (((1,), (1,)), ((), ())),
        preferred_element_type=jnp.float32,
    )
    plan_ref[...] = (found[:, 0:1] + found[:, 1:2] * slot_count).astype(jnp.int32)


def serve_rest(slots, ranks, rows, gates):
    slot_count, user_count = slots.shape
    (shard_rows, width), col_share = rows.shape, gates.shape[1]
    count = user_count - (user_count > 1)
    vmem = pl.BlockSpec(memory_space=pltpu.VMEM)
    return pl.pallas_call(
        functools.partial(serve_rest_kernel, user_count),
        out_shape=[jax.ShapeDtypeStruct((ranks.shape[1], 1), jnp.int32)]
        + [jax.ShapeDtypeStruct((slot_count, width), jnp.bfloat16)] * (count + 1),
        in_specs=[vmem] * 4,
        out_specs=[vmem] * (count + 2),
        compiler_params=pltpu.CompilerParams(vmem_limit_bytes=16 << 20),
        cost_estimate=pl.CostEstimate(
            flops=2 * count * slot_count * shard_rows * width,
            transcendentals=0,
            bytes_accessed=2 * shard_rows * col_share,
        ),
    )(slots, ranks, rows, gates)


def pick(plan, stride, slot_rows):
    slot_count, width = slot_rows[0].shape
    slot = lax.broadcasted_iota(jnp.int32, (plan.shape[0], slot_count), 1)
    total = jnp.zeros((plan.shape[0], width), jnp.float32)
    for k, rows in enumerate(slot_rows):
        total += jnp.dot(
            one_hot(slot == plan - k * stride), rows, preferred_element_type=jnp.float32
        )
    return total


def attention_kernel(group, user_count, length_ref, plan_ref, *refs):
    query_refs, out_ref = refs[:user_count], refs[-1]
    key_ref, value_ref, *event_refs = refs[user_count:-1]
    ctx, length = lax.axis_index("ctx"), length_ref[...]
    item_count, width = out_ref.shape
    plan = plan_ref[group * item_count : (group + 1) * item_count, :]
    stride = query_refs[0].shape[0]
    query = pick(plan, stride, [ref[:stride, :] for ref in query_refs]).astype(jnp.bfloat16)
    event_count = key_ref.shape[0]
    scale = 0.5 * HEAD ** (-0.5)
    scale_len = scale / length.astype(jnp.float32)
    for head in range(width // HEAD):
        cols = slice(head * HEAD, (head + 1) * HEAD)
        total = jnp.zeros((item_count, HEAD), jnp.float32)
        for k in range(len(event_refs) + 1):
            first = (ctx ^ k) * event_count
            for start in range(0, event_count, KEY_BLOCK):
                stop = min(start + KEY_BLOCK, event_count)
                if k == 0:
                    at = pl.ds(pl.multiple_of(ctx * width + head * HEAD, HEAD), HEAD)
                    key, value = key_ref[start:stop, at], value_ref[start:stop, at]
                else:
                    key = event_refs[k - 1][start:stop, cols]
                    value = event_refs[k - 1][event_count + start : event_count + stop, cols]
                place = first + start + lax.broadcasted_iota(jnp.int32, value.shape, 0)
                value = jnp.where(place < length, value, jnp.zeros_like(value))
                raw = lax.dot_general(
                    query[:, cols],
                    key,
                    (((1,), (1,)), ((), ())),
                    preferred_element_type=jnp.float32,
                )
                lead = raw * scale_len
                weights = (lead + lead * jnp.tanh(raw * scale)).astype(jnp.bfloat16)
                total += jnp.dot(weights, value, preferred_element_type=jnp.float32)
        out_ref[:, cols] = total.astype(out_ref.dtype)


def attend(length, plan, queries, keys, values, events, group, dtype):
    width = queries[0].shape[1]
    item_count = plan.shape[0] // (len(events) + 1)
    event_count = (len(events) + 1) * keys.shape[0]
    vmem = pl.BlockSpec(memory_space=pltpu.VMEM)
    operands = (length, plan, *queries, keys, values, *events)
    return pl.pallas_call(
        functools.partial(attention_kernel, group, len(queries)),
        out_shape=jax.ShapeDtypeStruct((item_count, width), dtype),
        in_specs=[vmem] * len(operands),
        out_specs=vmem,
        compiler_params=pltpu.CompilerParams(vmem_limit_bytes=24 << 20),
        cost_estimate=pl.CostEstimate(
            flops=4 * item_count * event_count * width,
            transcendentals=item_count * event_count * (width // HEAD),
            bytes_accessed=4 * event_count * width,
        ),
    )(*operands)


def gate_kernel(part_count, stride, plan_ref, *refs):
    attended_refs, gate_refs, out_ref = refs[:part_count], refs[part_count:-1], refs[-1]
    width = attended_refs[0].shape[1]
    item_count, count = out_ref.shape[0], stride // part_count
    for part, attended_ref in enumerate(attended_refs):
        starts = [ref.shape[0] - stride + part * count for ref in gate_refs]
        slots = [ref[at : at + count, :] for at, ref in zip(starts, gate_refs, strict=True)]
        gates = pick(plan_ref[:item_count, :], stride, slots)
        out_ref[:, part * width : (part + 1) * width] = (
            attended_ref[...].astype(jnp.float32) * gates
        ).astype(out_ref.dtype)


def gate(plan, attended, gates):
    item_count, width = attended[0].shape
    part_count = len(attended)
    vmem = pl.BlockSpec(memory_space=pltpu.VMEM)
    operands = (plan, *attended, *gates)
    return pl.pallas_call(
        functools.partial(gate_kernel, part_count, gates[0].shape[0]),
        out_shape=jax.ShapeDtypeStruct((item_count, part_count * width), jnp.bfloat16),
        in_specs=[vmem] * len(operands),
        out_specs=vmem,
        compiler_params=pltpu.CompilerParams(vmem_limit_bytes=16 << 20),
        cost_estimate=pl.CostEstimate(
            flops=2 * item_count * width * len(gates) * gates[0].shape[0],
            transcendentals=0,
            bytes_accessed=6 * item_count * width * part_count,
        ),
    )(*operands)


def project_kernel(head_count, part_count, *refs):
    pieces, weights = refs[:head_count], refs[head_count : 2 * head_count]
    out_ref = refs[-1]
    width = pieces[0].shape[1] // part_count
    chosen = []
    for ref in weights:
        for part in range(part_count):
            wanted = lax.axis_index("ctx") ^ part
            weight = ref[:width, :]
            for other in range(1, part_count):
                rows = slice(other * width, (other + 1) * width)
                weight = jnp.where(wanted == other, ref[rows, :], weight)
            chosen.append(weight)
    total = jnp.dot(
        jnp.concatenate([piece[...] for piece in pieces], axis=1),
        jnp.concatenate(chosen, axis=0),
        preferred_element_type=jnp.float32,
    )
    out_ref[...] = total.astype(out_ref.dtype)


def project_out(pieces, weights, part_count):
    item_count, width = pieces[0].shape
    cols = weights[0].shape[1]
    vmem = pl.BlockSpec(memory_space=pltpu.VMEM)
    operands = (*pieces, *weights)
    return pl.pallas_call(
        functools.partial(project_kernel, len(pieces), part_count),
        out_shape=jax.ShapeDtypeStruct((item_count, cols), jnp.bfloat16),
        in_specs=[vmem] * len(operands),
        out_specs=vmem,
        compiler_params=pltpu.CompilerParams(vmem_limit_bytes=16 << 20),
        cost_estimate=pl.CostEstimate(
            flops=2 * item_count * cols * width * len(pieces),
            transcendentals=0,
            bytes_accessed=2 * cols * width * len(pieces),
        ),
    )(*operands)


def head_split(catalog, cand_owner, cand_row, hist_len, proj_weight, keys, values, out_weight):
    user_count, ctx_count = lax.axis_size("user"), lax.axis_size("ctx")
    head_count = lax.axis_size("head")
    head = lax.axis_index("head")
    shard_rows, model_width = catalog.shape
    col_share = proj_weight.shape[2]
    width = col_share // ctx_count
    cand_count = cand_row.shape[1]
    slot_count = ctx_count * (2 * cand_count // user_count)
    key_rows, value_rows = keys[0], values[0]
    length = hist_len.reshape(1, 1)

    ids = cand_owner[0].reshape(1, cand_count) * shard_rows + cand_row
    others = [swap(ids, "ctx", k) for k in range(1, ctx_count)]
    pieces, step = [jnp.concatenate([ids, *others], axis=1)], 1
    while step < user_count:
        pieces.append(swap(jnp.concatenate(pieces, axis=0), "user", step))
        step *= 2

    events = []
    for k in range(1, ctx_count):
        part = split_events(key_rows, value_rows, width, k)
        events.append(swap(part, "ctx", k))

    weight = proj_weight.reshape(model_width, 2 * col_share)
    rows, gate_rows = project_shard(catalog, weight, width)
    slots, ranks, *served = serve(pieces, rows, gate_rows, slot_count, width)
    order = range(user_count - 1, 0, -1)
    fetched = {k: swap(served[k - 1], "user", k) for k in order}
    plan, query, *served = serve_rest(slots, ranks, rows, gate_rows)
    queries = [query] + [fetched[k] for k in range(1, user_count)]
    fetched = {k: swap(served[k - 1], "user", k) for k in order if k > 1}
    gates = [served[0], *queries[1:2]] + [fetched[k] for k in range(2, user_count)]

    weights = [columns_of(out_weight, head * col_share, col_share)]
    for j in range(1, head_count):
        part = columns_of(out_weight, (head ^ j) * col_share, col_share)
        weights.append(swap(part, "head", j))

    attended = [None] * ctx_count
    for k in range(ctx_count - 1, -1, -1):
        own = attend(
            length, plan, queries, key_rows, value_rows, events, k, jnp.bfloat16 if k else jnp.float32
        )
        attended[k] = swap(own, "ctx", k) if k > 0 else own

    gated = gate(plan, attended, gates)
    parts, bit = {0: gated}, head_count // 2
    while bit:
        for j in list(parts):
            parts[j ^ bit] = swap(parts[j], "head", bit)
        bit //= 2
    heads = range(head_count)
    ranked = project_out([parts[j] for j in heads], [weights[j] for j in heads], ctx_count)
    return ranked.reshape(1, cand_count, col_share)


def whole_heads(mesh, proj_weight):
    sizes = [mesh.shape[a] for a in ("user", "ctx", "head")]
    heads = proj_weight.shape[2] // mesh.shape["head"] // HEAD
    return all(n & (n - 1) == 0 for n in sizes) and heads % mesh.shape["ctx"] == 0 and sizes[0] > 1


def solution(mesh):
    def step(per_device):
        return jax.shard_map(
            per_device,
            mesh=mesh,
            in_specs=(
                P("user", None),
                P("user", "ctx", None),
                P("user", "ctx"),
                P("user"),
                P(None, None, "head"),
                P("user", "ctx", "head"),
                P("user", "ctx", "head"),
                P("head", None),
            ),
            out_specs=P("user", "ctx", "head"),
            check_vma=False,
        )

    def run(catalog, cand_owner, cand_row, hist_len, proj_weight, keys, values, out_weight):
        args = (catalog, cand_owner, cand_row, hist_len, proj_weight, keys, values, out_weight)
        if not whole_heads(mesh, proj_weight):
            return step(event_split)(*args)
        return step(head_split)(*args)

    return run
```
